128 devices in a mesh: dev: 32 (over z, x, core), rep: 4 (over y).
Axes of the slice: x: 4, y: 4, z: 4, core: 2. Of those that a mesh axis runs over, the one named last changes fastest.
Arguments:
- emb_table: float32 [131072, 160], P('dev'), may hold values from -6 to 6
- feature_ids: int32 [16384, 4, 8], P(('dev', 'rep')), may hold values from 0 to 32767
- lengths: int32 [16384, 4], P(('dev', 'rep')), may hold values from 1 to 8
- cotangent: float32 [16384, 4, 160], P(('dev', 'rep')), may hold values from -6 to 6
Outputs:
- pooled: float32 [16384, 4, 160], P(('dev', 'rep'))
- row_grads: float32 [131072, 160], P(('dev', 'rep'))
The draws below stay inside these ranges and needn't reach their ends.
All inputs are finite; a program needn't handle non-finite values.
Results may differ from the reference program's by a relative error of at most 0.00008.
Values sent between devices are 32-bit elements; how exact they have to be, the bound alone decides.
No kernel may reach another device: no remote copies, remote signals or barrier semaphores. Data moves between devices by JAX's collectives and lax.ppermute only.
A program may use at most 128 MiB of HBM per device.

```python
import math
import jax
import jax.numpy as jnp
import numpy as np
from jax import lax

E = 160
FEATS = 4
BAG = 8
ROWS_DEV = 4096
ROWS = 131072
VOCAB = 32768
BATCH = 16384
N_DEV = 32


def touch_ends(entries, rng, low, largest):
    place = [jax.random.randint(jax.random.fold_in(rng, axis), (), 0, length) for axis, length in enumerate(entries.shape)]
    longest = entries.shape.index(max(entries.shape))
    beside = place[:longest] + [(place[longest] + 1) % entries.shape[longest]] + place[longest + 1:]
    return entries.at[tuple(place)].set(low).at[tuple(beside)].set(largest)


def steps_of(key, dims, pieces, smallest, high):
    loudness, own = 1.0, jax.random.fold_in(key, 6)
    for axis_at, blocks in pieces:
        draws = jnp.exp(jax.random.uniform(jax.random.fold_in(own, axis_at), (blocks,), jnp.float32, smallest / len(pieces), high / len(pieces)))
        loudness = loudness * jnp.repeat(draws, dims[axis_at] // blocks).reshape([-1 if axis == axis_at else 1 for axis in range(len(dims))])
    return loudness


def rank_table(amount, skew):
    loads = [(1 << 20) // math.isqrt(rank ** skew) + 1 for rank in range(1, amount + 1)]
    deviation = 1 + sum(loads) // (1 << 30)
    return np.cumsum(np.array([max(1, weight // deviation) for weight in loads]))


def ranked(stream_key, shape, count, lean):
    grid = rank_table(count, lean)
    ticket = jax.random.randint(jax.random.fold_in(stream_key, 1), shape, 0, int(grid[count - 1]))
    grade = jnp.searchsorted(jnp.asarray(grid, jnp.int32), ticket, side="right")
    return jax.random.permutation(jax.random.fold_in(stream_key, 2), count)[grade].astype(jnp.int32)


def centred(key, dims, deviation, limit, split=(), held_as=jnp.bfloat16):
    drawn = deviation * jax.random.normal(key, dims, jnp.float32)
    if split:
        drawn = drawn * steps_of(key, dims, split, -0.22, 0.18)
    return jnp.clip(drawn, -limit, limit).astype(held_as)


def setup_inputs(seed: int = 0) -> dict:
    key_list = jax.random.split(jax.random.key(seed), 5)
    return {
        "emb_table": centred(key_list[0], (ROWS, E), 1.0, 6.0, ((0, 32),), jnp.float32),
        "feature_ids": touch_ends(ranked(key_list[1], (BATCH, FEATS, BAG), VOCAB, 2), jax.random.fold_in(key_list[1], 3), 0, VOCAB - 1).astype(jnp.int32),
        "lengths": touch_ends(jax.random.randint(key_list[2], (BATCH, FEATS), 1, BAG + 1), jax.random.fold_in(key_list[2], 1), 1, BAG).astype(jnp.int32),
        "cotangent": centred(key_list[3], (BATCH, FEATS, E), 1.0, 6.0, ((0, 128),), jnp.float32),
    }


def reference(emb_table, feature_ids, lengths, cotangent):
    vocabulary = ROWS_DEV * N_DEV // FEATS
    slot_index = jnp.arange(BAG, dtype=jnp.int32)
    live_slots = slot_index[None, None, :] < lengths[:, :, None]
    share = 1.0 / lengths.astype(jnp.float32)
    weights = jnp.where(live_slots, share[:, :, None], 0.0).astype(jnp.float32)
    offsets = (jnp.arange(FEATS, dtype=jnp.int32) * vocabulary).astype(jnp.int32)
    global_ids = (feature_ids + offsets[None, :, None]).astype(jnp.int32)

    def pool_feature(inputs):
        feature_rows, feature_weights = inputs
        gathered = emb_table[feature_rows]
        return jnp.sum(gathered * feature_weights[:, :, None], axis=1)

    pooled = lax.map(pool_feature, (jnp.transpose(global_ids, (1, 0, 2)), jnp.transpose(weights, (1, 0, 2))))
    pooled = jnp.transpose(pooled, (1, 0, 2))

    def add_feature(running, inputs):
        feature_rows, feature_weights, feature_cot = inputs
        contrib = feature_weights[:, :, None] * feature_cot[:, None, :]
        running = running.at[feature_rows.reshape(-1)].add(contrib.reshape(-1, E))
        return running, None

    start_grads = jnp.zeros((ROWS_DEV * N_DEV, E), jnp.float32)
    row_grads, _ = lax.scan(add_feature, start_grads, (jnp.transpose(global_ids, (1, 0, 2)), jnp.transpose(weights, (1, 0, 2)), jnp.transpose(cotangent, (1, 0, 2))))
    return pooled, row_grads
```

```python
import functools
import jax, jax.numpy as jnp
from jax import lax
from jax.experimental import pallas as pl
from jax.experimental.pallas import tpu as pltpu
from jax.sharding import PartitionSpec as P

LOW = 64
BF = jnp.bfloat16
F32 = jnp.float32


def split_store(dst, cols, x):
    width = x.shape[0]
    high = x.astype(BF)
    dst[0:width, cols] = high
    dst[width : 2 * width, cols] = (x - high.astype(F32)).astype(BF)


def make_keys(base, rows_dev, ids_ref, key_low, key_high, key_count, depth_ref):
    bag = ids_ref.shape[1]
    own, low, valid, lead = [], [], [], []
    for j in range(bag):
        shifted = ids_ref[:, j, :] - base
        good = jnp.logical_and(ids_ref[:, j, :] >= 0, jnp.logical_and(shifted >= 0, shifted < rows_dev))
        own.append(jnp.where(good, shifted, -1))
        low.append(shifted & (LOW - 1))
        valid.append(good)
    deepest = jnp.zeros(own[0].shape, jnp.int32)
    for j in range(bag):
        fresh = valid[j]
        for k in range(j):
            fresh = jnp.logical_and(fresh, own[k] != own[j])
        lead.append(fresh)
    for j in range(bag):
        count = jnp.ones(own[0].shape, F32)
        for k in range(j + 1, bag):
            count = count + jnp.where(own[k] == own[j], 1.0, 0.0)
        level = jnp.zeros(own[0].shape, jnp.int32)
        for k in range(j):
            level = level + jnp.where(jnp.logical_and(lead[k], low[k] == low[j]), 1, 0)
        key_low[j] = jnp.where(lead[j], low[j] + LOW * level, -1)
        key_high[j] = (own[j] >> (LOW.bit_length() - 1)).astype(F32)
        key_count[j] = count
        deepest = jnp.maximum(deepest, jnp.where(lead[j], level + 1, 0))
    depth_ref[0] = jnp.max(deepest)

    @pl.when(depth_ref[0] > 2)
    def _():
        for s in range(deepest.shape[0]):
            depth_ref[1 + s] = jnp.max(deepest[s : s + 1])


def layer_of(source, depth, key_low, key_high, key_count):
    bag = key_low.shape[0]
    place = lax.broadcasted_iota(jnp.int32, (LOW, 128), 0) + LOW * depth
    high = jnp.full((LOW, 128), -1.0, F32)
    count = jnp.zeros((LOW, 128), F32)
    for j in range(bag):
        hit = jnp.broadcast_to(key_low[j, pl.ds(source, 1), :], (LOW, 128)) == place
        high = jnp.where(hit, jnp.broadcast_to(key_high[j, pl.ds(source, 1), :], (LOW, 128)), high)
        count = jnp.where(hit, jnp.broadcast_to(key_count[j, pl.ds(source, 1), :], (LOW, 128)), count)
    return high.astype(BF), count.astype(BF)


def counts_for(block, layers):
    want = jnp.asarray(block, F32).astype(BF)
    tile = jnp.zeros((LOW, 128), BF)
    for high, count in layers:
        tile = jnp.where(high == want, count, tile)
    return tile


def pool_kernel(per_step, base_ref, ids_ref, table_ref, out_ref, highs_ref, counts_ref,
                parts, key_low, key_high, key_count, depth_ref):
    step = pl.program_id(0)
    width, rows_dev = table_ref.shape

    @pl.when(step == 0)
    def _():
        for c in range(0, rows_dev, 512):
            split_store(parts, pl.ds(c, 512), table_ref[:, c : c + 512])
        make_keys(base_ref[0], rows_dev, ids_ref, key_low, key_high, key_count, depth_ref)

    layers = []
    for s in range(per_step):
        source = step * per_step + s
        pair = [layer_of(source, depth, key_low, key_high, key_count) for depth in range(2)]
        for depth in range(2):
            highs_ref[depth, s] = pair[depth][0]
            counts_ref[depth, s] = pair[depth][1]
        layers.append(pair)
    chunk = 512
    total = jnp.zeros((2 * width, 128 * per_step), F32)
    for c in range(0, rows_dev, chunk):
        tile = jnp.concatenate(
            [jnp.concatenate([counts_for(c // LOW + h, layers[s]) for h in range(chunk // LOW)], axis=0)
             for s in range(per_step)], axis=1)
        total = total + jnp.dot(parts[:, c : c + chunk], tile, preferred_element_type=F32)
    for s in range(per_step):
        cols = slice(128 * s, 128 * s + 128)
        out_ref[s] = total[0:width, cols] + total[width : 2 * width, cols]

    @pl.when(depth_ref[0] > 2)
    def _():
        for s in range(per_step):
            source = step * per_step + s

            def deeper(depth, carry):
                extra = layer_of(source, depth, key_low, key_high, key_count)

                def add(block, value):
                    tile = jnp.concatenate(
                        [counts_for(block * (128 // LOW) + h, [extra]) for h in range(128 // LOW)], axis=0)
                    return value + jnp.dot(parts[:, pl.ds(pl.multiple_of(block * 128, 128), 128)],
                                           tile, preferred_element_type=F32)

                more = lax.fori_loop(0, rows_dev // 128, add, jnp.zeros((2 * width, 128), F32))
                out_ref[s] += more[0:width] + more[width : 2 * width]
                return carry

            lax.fori_loop(2, depth_ref[1 + source], deeper, 0)


def pool(base, ids, table_t):
    sources, bag, _ = ids.shape
    width, rows_dev = table_t.shape
    per_step = 2
    full = lambda *shape: pl.BlockSpec(shape, lambda i: (0,) * len(shape))
    return pl.pallas_call(
        functools.partial(pool_kernel, per_step),
        grid=(sources // per_step,),
        in_specs=[pl.BlockSpec(memory_space=pltpu.SMEM), full(sources, bag, 128), full(width, rows_dev)],
        out_specs=[
            pl.BlockSpec((per_step, width, 128), lambda i: (i, 0, 0)),
            pl.BlockSpec((2, per_step, LOW, 128), lambda i: (0, i, 0, 0)),
            pl.BlockSpec((2, per_step, LOW, 128), lambda i: (0, i, 0, 0)),
        ],
        out_shape=[
            jax.ShapeDtypeStruct((sources, width, 128), F32),
            jax.ShapeDtypeStruct((2, sources, LOW, 128), BF),
            jax.ShapeDtypeStruct((2, sources, LOW, 128), BF),
        ],
        scratch_shapes=[
            pltpu.VMEM((2 * width, rows_dev), BF),
            pltpu.VMEM((bag, sources, 128), jnp.int32),
            pltpu.VMEM((bag, sources, 128), F32),
            pltpu.VMEM((bag, sources, 128), F32),
            pltpu.SMEM((1 + sources,), jnp.int32),
        ],
        compiler_params=pltpu.CompilerParams(dimension_semantics=("arbitrary",)),
        name="pool",
    )(base, ids, table_t)


def grad_kernel(first, blk, rows_dev, base_ref, ids_ref, scaled_ref, highs_ref, counts_ref, out_ref,
                parts, key_low, key_high, key_count, depth_ref):
    step = pl.program_id(0)
    sources, width, _ = scaled_ref.shape

    @pl.when(step == 0)
    def _():
        for s in range(sources):
            split_store(parts, pl.ds(128 * s, 128), scaled_ref[s])
        make_keys(base_ref[0], rows_dev, ids_ref, key_low, key_high, key_count, depth_ref)

    start = (first + step) * (blk // LOW)
    together = 4
    total = jnp.zeros((2 * width, blk), F32)
    for s in range(0, sources, together):
        tile = jnp.concatenate(
            [jnp.concatenate([counts_for(start + h, [(highs_ref[d, s + t], counts_ref[d, s + t]) for d in range(2)])
                              for h in range(blk // LOW)], axis=0)
             for t in range(together)], axis=1)
        total = total + lax.dot_general(parts[:, 128 * s : 128 * (s + together)], tile,
                                        (((1,), (1,)), ((), ())), preferred_element_type=F32)
    out_ref[...] = total[0:width] + total[width : 2 * width]

    @pl.when(depth_ref[0] > 2)
    def _():
        def visit(s, carry):
            def deeper(depth, carry):
                extra = layer_of(s, depth, key_low, key_high, key_count)
                tile = jnp.concatenate([counts_for(start + h, [extra]) for h in range(blk // LOW)], axis=0)
                more = lax.dot_general(parts[:, pl.ds(pl.multiple_of(s * 128, 128), 128)], tile,
                                       (((1,), (1,)), ((), ())), preferred_element_type=F32)
                out_ref[...] += more[0:width] + more[width : 2 * width]
                return carry

            return lax.fori_loop(2, depth_ref[1 + s], deeper, carry)

        lax.fori_loop(0, sources, visit, 0)


def grads(base, ids, scaled, highs, counts, rows_dev, groups, first=0, n=16, blk=256):
    sources, bag, _ = ids.shape
    width = scaled.shape[1]
    full = lambda *shape: pl.BlockSpec(shape, lambda i: (0,) * len(shape))
    return pl.pallas_call(
        functools.partial(grad_kernel, first, blk, rows_dev),
        grid=(n,),
        in_specs=[pl.BlockSpec(memory_space=pltpu.SMEM), full(sources, bag, 128), full(sources, width, 128),
                  full(2, sources, LOW, 128), full(2, sources, LOW, 128)],
        out_specs=pl.BlockSpec((None, width, blk), lambda i: (i // (n // groups), 0, i % (n // groups))),
        out_shape=jax.ShapeDtypeStruct((groups, width, n // groups * blk), F32),
        scratch_shapes=[
            pltpu.VMEM((2 * width, sources * 128), BF),
            pltpu.VMEM((bag, sources, 128), jnp.int32),
            pltpu.VMEM((bag, sources, 128), F32),
            pltpu.VMEM((bag, sources, 128), F32),
            pltpu.SMEM((1 + sources,), jnp.int32),
        ],
        compiler_params=pltpu.CompilerParams(dimension_semantics=("arbitrary",)),
        name="grads",
    )(base, ids, scaled, highs, counts)


def to_all(x, axis):
    return lax.all_to_all(x, axis, split_axis=0, concat_axis=0, tiled=True)


def body(emb_table, feature_ids, lengths, cotangent):
    dev_count = lax.axis_size("dev")
    rep_count = lax.axis_size("rep")
    rows_dev, width = emb_table.shape
    examples, features, bag = feature_ids.shape
    owners_each = dev_count // features
    base = (lax.axis_index("dev") % owners_each * rows_dev).astype(jnp.int32).reshape(1)

    ids_t = jnp.transpose(feature_ids, (1, 2, 0))
    share = 1.0 / jnp.transpose(lengths, (1, 0)).astype(F32)
    slot = lax.broadcasted_iota(jnp.int32, ids_t.shape, 1)
    masked = jnp.where(slot < jnp.transpose(lengths, (1, 0))[:, None, :], ids_t, -1)
    ids = to_all(jnp.repeat(masked, owners_each, axis=0), "dev")
    scaled = jnp.transpose(cotangent, (1, 2, 0)) * share[:, None, :]
    scaled_all = to_all(jnp.repeat(scaled, owners_each, axis=0), "dev")
    partial, highs, counts = pool(base, ids, jnp.transpose(emb_table))
    pooled = to_all(partial, "dev").reshape(features, owners_each, width, examples)
    pooled = jnp.sum(pooled, axis=1) * share[:, None, :]
    blocks = grads(base, ids, scaled_all, highs, counts, rows_dev, rep_count)
    row_grads = jnp.sum(to_all(blocks, "rep"), axis=0)
    return jnp.transpose(pooled, (2, 0, 1)), jnp.transpose(row_grads)


def solution(mesh):
    return jax.shard_map(
        body,
        mesh=mesh,
        in_specs=(
            P("dev", None),
            P(("dev", "rep"), None, None),
            P(("dev", "rep"), None),
            P(("dev", "rep"), None, None),
        ),
        out_specs=(P(("dev", "rep"), None, None), P(("dev", "rep"), None)),
        check_vma=False,
    )
```

```python
import functools

import jax
import jax.numpy as jnp
from jax import lax
from jax.experimental import pallas as pl
from jax.experimental.pallas import tpu as pltpu
from jax.sharding import Mesh
from jax.sharding import PartitionSpec as P

LOW = 128
LANES = 128
BF = jnp.bfloat16
F32 = jnp.float32
I32 = jnp.int32
WHOLE = pl.BlockSpec(memory_space=pltpu.VMEM)
SCALARS = pl.BlockSpec(memory_space=pltpu.SMEM)


def split_store(dst, cols, x):
    width = x.shape[0]
    high = x.astype(BF)
    dst[0:width, cols] = high
    dst[width : 2 * width, cols] = (x - high.astype(F32)).astype(BF)


def split_table(table_t):
    width, rows = table_t.shape
    step = 1024

    def kernel(x_ref, out_ref):
        for c in range(0, step, 512):
            split_store(out_ref, slice(c, c + 512), x_ref[:, c : c + 512])

    return pl.pallas_call(
        kernel,
        grid=(rows // step,),
        in_specs=[pl.BlockSpec((width, step), lambda i: (0, i))],
        out_specs=pl.BlockSpec((2 * width, step), lambda i: (0, i)),
        out_shape=jax.ShapeDtypeStruct((2 * width, rows), BF),
        name="split_table",
    )(table_t)


def split_blocks(blocks):
    sources, width, lanes = blocks.shape
    step = 4

    def kernel(x_ref, out_ref):
        for s in range(step):
            split_store(out_ref, slice(s * lanes, (s + 1) * lanes), x_ref[s])

    return pl.pallas_call(
        kernel,
        grid=(sources // step,),
        in_specs=[pl.BlockSpec((step, width, lanes), lambda i: (i, 0, 0))],
        out_specs=pl.BlockSpec((2 * width, step * lanes), lambda i: (0, i)),
        out_shape=jax.ShapeDtypeStruct((2 * width, sources * lanes), BF),
        name="split_blocks",
    )(blocks)


def make_keys(base, rows_dev, ids_ref, key_low, key_high, key_count):
    bag = ids_ref.shape[1]
    own, low, lead = [], [], []
    for j in range(bag):
        ids = ids_ref[:, j, :]
        shifted = ids - base
        good = jnp.logical_and(ids >= 0, jnp.logical_and(shifted >= 0, shifted < rows_dev))
        own.append(jnp.where(good, shifted, -1))
        low.append(shifted & (LOW - 1))
        fresh = good
        for k in range(j):
            fresh = jnp.logical_and(fresh, own[k] != own[j])
        lead.append(fresh)
    deepest = jnp.zeros(own[0].shape, I32)
    for j in range(bag):
        count = jnp.ones(own[0].shape, F32)
        for k in range(j + 1, bag):
            count = count + jnp.where(own[k] == own[j], 1.0, 0.0)
        level = jnp.zeros(own[0].shape, I32)
        for k in range(j):
            level = level + jnp.where(jnp.logical_and(lead[k], low[k] == low[j]), 1, 0)
        key_low[j] = jnp.where(lead[j], low[j] + LOW * level, -1).astype(F32)
        key_high[j] = (own[j] >> (LOW.bit_length() - 1)).astype(F32)
        key_count[j] = count
        deepest = jnp.maximum(deepest, jnp.where(lead[j], level + 1, 0))
    return deepest


def spread(ref, j, source):
    return jnp.broadcast_to(ref[j, pl.ds(source, 1), :], (16, LANES)).astype(BF)


def first_layers(source, key_low, key_high, key_count):
    bag = key_low.shape[0]
    lows = [spread(key_low, j, source) for j in range(bag)]
    highs = [spread(key_high, j, source) for j in range(bag)]
    counts = [spread(key_count, j, source) for j in range(bag)]
    sub = lax.broadcasted_iota(I32, (16, LANES), 0).astype(F32)
    layers = []
    for depth in range(2):
        high_rows, count_rows = [], []
        for group in range(LOW // 16):
            place = (sub + float(LOW * depth + 16 * group)).astype(BF)
            high = jnp.full((16, LANES), -1.0, BF)
            count = jnp.zeros((16, LANES), BF)
            for j in range(bag):
                hit = lows[j] == place
                high = jnp.where(hit, highs[j], high)
                count = jnp.where(hit, counts[j], count)
            high_rows.append(high)
            count_rows.append(count)
        layers.append((jnp.concatenate(high_rows, axis=0), jnp.concatenate(count_rows, axis=0)))
    return layers


def deep_layer(source, depth, key_low, key_high, key_count):
    bag = key_low.shape[0]
    place = (lax.broadcasted_iota(I32, (LOW, LANES), 0) + LOW * depth).astype(F32)
    high = jnp.full((LOW, LANES), -1.0, F32)
    count = jnp.zeros((LOW, LANES), F32)
    for j in range(bag):
        hit = jnp.broadcast_to(key_low[j, pl.ds(source, 1), :], (LOW, LANES)) == place
        high = jnp.where(hit, jnp.broadcast_to(key_high[j, pl.ds(source, 1), :], (LOW, LANES)), high)
        count = jnp.where(hit, jnp.broadcast_to(key_count[j, pl.ds(source, 1), :], (LOW, LANES)), count)
    return high.astype(BF), count.astype(BF)


def counts_for(block, layers):
    want = jnp.asarray(block, F32).astype(BF)
    tile = jnp.zeros((LOW, LANES), BF)
    for high, count in layers:
        tile = jnp.where(high == want, count, tile)
    return tile


def pool_kernel(per_step, base_ref, ids_ref, parts_ref, out_ref, highs_ref, counts_ref, depth_ref,
                key_low, key_high, key_count):
    step = pl.program_id(0)
    width = out_ref.shape[1]
    rows_dev = parts_ref.shape[1]
    sources = ids_ref.shape[0]

    def build(at):
        for s in range(per_step):
            layers = first_layers(at * per_step + s, key_low, key_high, key_count)
            for depth in range(2):
                highs_ref[depth, at * per_step + s] = layers[depth][0]
                counts_ref[depth, at * per_step + s] = layers[depth][1]

    @pl.when(step == 0)
    def _():
        deepest = make_keys(base_ref[0], rows_dev, ids_ref, key_low, key_high, key_count)
        depth_ref[0] = jnp.max(deepest)

        @pl.when(depth_ref[0] > 2)
        def _():
            for s in range(sources):
                depth_ref[1 + s] = jnp.max(deepest[s : s + 1])

        build(0)

    layers = [[(highs_ref[depth, step * per_step + s], counts_ref[depth, step * per_step + s])
               for depth in range(2)] for s in range(per_step)]
    chunk = 512
    total = jnp.zeros((2 * width, LANES * per_step), F32)
    for c in range(0, rows_dev, chunk):
        tile = jnp.concatenate(
            [jnp.concatenate([counts_for(c // LOW + h, layers[s]) for h in range(chunk // LOW)], axis=0)
             for s in range(per_step)], axis=1)
        total = total + jnp.dot(parts_ref[:, c : c + chunk], tile, preferred_element_type=F32)
    for s in range(per_step):
        cols = slice(LANES * s, LANES * (s + 1))
        out_ref[s] = total[0:width, cols] + total[width : 2 * width, cols]

    build(jnp.minimum(step + 1, sources // per_step - 1))

    @pl.when(depth_ref[0] > 2)
    def _():
        for s in range(per_step):
            source = step * per_step + s

            def deeper(depth, carry):
                extra = deep_layer(source, depth, key_low, key_high, key_count)
                wide = 4 * LOW

                def add(block, value):
                    tile = jnp.concatenate([counts_for(block * (wide // LOW) + h, [extra])
                                            for h in range(wide // LOW)], axis=0)
                    return value + jnp.dot(parts_ref[:, pl.ds(pl.multiple_of(block * wide, wide), wide)],
                                           tile, preferred_element_type=F32)

                more = lax.fori_loop(0, rows_dev // wide, add, jnp.zeros((2 * width, LANES), F32))
                out_ref[s] += more[0:width] + more[width : 2 * width]
                return carry

            lax.fori_loop(2, depth_ref[1 + source], deeper, 0)


def pool(base, ids, parts):
    sources, bag, _ = ids.shape
    width, rows_dev = parts.shape[0] // 2, parts.shape[1]
    per_step = 2
    keys = pltpu.VMEM((bag, sources, LANES), F32)
    layer = jax.ShapeDtypeStruct((2, sources, LOW, LANES), BF)
    return pl.pallas_call(
        functools.partial(pool_kernel, per_step),
        grid=(sources // per_step,),
        in_specs=[SCALARS, WHOLE, WHOLE],
        out_specs=[pl.BlockSpec((per_step, width, LANES), lambda i: (i, 0, 0)), WHOLE, WHOLE, SCALARS],
        out_shape=[
            jax.ShapeDtypeStruct((sources, width, LANES), F32),
            layer,
            layer,
            jax.ShapeDtypeStruct((1 + sources,), I32),
        ],
        scratch_shapes=[keys, keys, keys],
        compiler_params=pltpu.CompilerParams(dimension_semantics=("arbitrary",)),
        name="pool",
    )(base, ids, parts)


def grad_kernel(blk, rows_dev, base_ref, first_ref, *refs):
    halves = [refs[0:5], refs[5:10]]
    top_ref, bottom_ref, key_low, key_high, key_count = refs[10:]
    half = top_ref.shape[0]
    width = 2 * half
    start = first_ref[0] + pl.program_id(0) * (blk // LOW)
    together = 4
    total = jnp.zeros((2 * width, blk), F32)
    for ids_ref, parts_ref, highs_ref, counts_ref, depth_ref in halves:
        for s in range(0, ids_ref.shape[0], together):
            tile = jnp.concatenate(
                [jnp.concatenate([counts_for(start + h, [(highs_ref[d, s + t], counts_ref[d, s + t]) for d in range(2)])
                                  for h in range(blk // LOW)], axis=0)
                 for t in range(together)], axis=1)
            total = total + lax.dot_general(parts_ref[:, LANES * s : LANES * (s + together)], tile,
                                            (((1,), (1,)), ((), ())), preferred_element_type=F32)
    top_ref[...] = total[0:half] + total[width : width + half]
    bottom_ref[...] = total[half:width] + total[width + half :]

    for ids_ref, parts_ref, highs_ref, counts_ref, depth_ref in halves:
        @pl.when(depth_ref[0] > 2)
        def _():
            make_keys(base_ref[0], rows_dev, ids_ref, key_low, key_high, key_count)

            def visit(s, carry):
                def deeper(depth, inner):
                    extra = deep_layer(s, depth, key_low, key_high, key_count)
                    tile = jnp.concatenate([counts_for(start + h, [extra]) for h in range(blk // LOW)], axis=0)
                    more = lax.dot_general(parts_ref[:, pl.ds(pl.multiple_of(s * LANES, LANES), LANES)], tile,
                                           (((1,), (1,)), ((), ())), preferred_element_type=F32)
                    top_ref[...] += more[0:half] + more[width : width + half]
                    bottom_ref[...] += more[half:width] + more[width + half :]
                    return inner

                return lax.fori_loop(2, depth_ref[1 + s], deeper, carry)

            lax.fori_loop(0, ids_ref.shape[0], visit, 0)


def grads(base, first_row, rows, rows_dev, own, other):
    sources, bag, _ = own[0].shape
    width = own[1].shape[0] // 2
    blk = 256
    keys = pltpu.VMEM((bag, sources, LANES), F32)
    out = pl.BlockSpec((width // 2, blk), lambda i: (0, i))
    each = [WHOLE, WHOLE, WHOLE, WHOLE, SCALARS]
    return pl.pallas_call(
        functools.partial(grad_kernel, blk, rows_dev),
        grid=(rows // blk,),
        in_specs=[SCALARS, SCALARS] + each + each,
        out_specs=[out, out],
        out_shape=[jax.ShapeDtypeStruct((width // 2, rows), F32)] * 2,
        scratch_shapes=[keys, keys, keys],
        compiler_params=pltpu.CompilerParams(dimension_semantics=("arbitrary",)),
        name="grads",
    )(base, (first_row // LOW).astype(I32).reshape(1), *own, *other)


def to_all(x, axis):
    return lax.all_to_all(x, axis, split_axis=0, concat_axis=0, tiled=True)


def shifted(x, axis, by):
    n = lax.axis_size(axis)
    return lax.ppermute(x, axis, [(i, (i + by) % n) for i in range(n)])


def body(emb_table, feature_ids, lengths, cotangent):
    rows_dev, width = emb_table.shape
    examples, features, bag = feature_ids.shape
    chips = lax.axis_size("x")
    cores = lax.axis_size("core")
    reps = lax.axis_size("rep")
    core = lax.axis_index("core")
    rep = lax.axis_index("rep")
    base = ((lax.axis_index("x") * cores + core) * rows_dev).astype(I32).reshape(1)

    ids_t = jnp.transpose(feature_ids, (1, 2, 0))
    lengths_t = jnp.transpose(lengths, (1, 0))
    share = 1.0 / lengths_t.astype(F32)
    slot = lax.broadcasted_iota(I32, ids_t.shape, 1)
    masked = jnp.where(slot < lengths_t[:, None, :], ids_t, -1)
    ids = to_all(jnp.repeat(masked, chips * cores, axis=0), ("z", "x", "core"))
    ids = ids.reshape(features * chips, cores, bag, examples)
    ids_own = lax.dynamic_index_in_dim(ids, core, 1, keepdims=False)
    ids_other = lax.dynamic_index_in_dim(ids, 1 - core, 1, keepdims=False)

    scaled = jnp.transpose(cotangent, (1, 2, 0)) * share[:, None, :]
    scaled_own = to_all(jnp.repeat(scaled, chips, axis=0), ("z", "x"))
    scaled_other = shifted(scaled_own, "core", 1)

    parts = split_table(jnp.transpose(emb_table))
    sent, *layers_other = pool(base, ids_other, parts)
    kept, *layers_own = pool(base, ids_own, parts)
    partial = kept + shifted(sent, "core", 1)
    pooled = to_all(partial, ("z", "x")).reshape(features, chips, width, examples)
    pooled = jnp.sum(pooled, axis=1) * share[:, None, :]

    own = [ids_own, split_blocks(scaled_own), *layers_own]
    other = [ids_other, split_blocks(scaled_other), *layers_other]
    rows = rows_dev // reps

    def block(ahead):
        return grads(base, (rep + ahead) % reps * rows, rows, rows_dev, own, other)

    far_top, far_bottom = block(2)
    from_left = shifted(far_top, "rep", 1)
    from_right = shifted(far_bottom, "rep", -1)
    next_top, next_bottom = block(1)
    prev_top, prev_bottom = block(reps - 1)
    got_bottom = shifted(next_bottom, "rep", 1)
    got_top = shifted(prev_top, "rep", -1)
    got_left_top = shifted(next_top + from_left, "rep", 1)
    got_right_bottom = shifted(prev_bottom + from_right, "rep", -1)
    here_top, here_bottom = block(0)
    row_grads = jnp.concatenate(
        [here_top + got_top + got_left_top, here_bottom + got_bottom + got_right_bottom], axis=0
    )
    return jnp.transpose(pooled, (2, 0, 1)), jnp.transpose(row_grads)


def solution(mesh):
    devices = mesh.devices.reshape(4, 4, 2, mesh.shape["rep"])
    fine = Mesh(devices, ("z", "x", "core", "rep"))
    dev = ("z", "x", "core")
    every = ("z", "x", "core", "rep")
    return jax.shard_map(
        body,
        mesh=fine,
        in_specs=(P(dev, None), P(every, None, None), P(every, None), P(every, None, None)),
        out_specs=(P(every, None, None), P(every, None)),
        check_vma=False,
    )
```

```python
import functools

import jax
import jax.numpy as jnp
from jax import lax
from jax.experimental import pallas as pl
from jax.experimental.pallas import tpu as pltpu
from jax.sharding import Mesh
from jax.sharding import PartitionSpec as P


LOW = 64
GRANT = 20 * 1024 * 1024
LANES = 128
BF = jnp.bfloat16
F32 = jnp.float32
I32 = jnp.int32
WHOLE = pl.BlockSpec(memory_space=pltpu.VMEM)
SCALARS = pl.BlockSpec(memory_space=pltpu.SMEM)


def two_parts(x):
    high = lax.reduce_precision(x, exponent_bits=8, mantissa_bits=7)
    return high.astype(BF), (x - high).astype(BF)


def estimate(width, rows, columns):
    flops = 4 * width * rows * columns
    return pl.CostEstimate(flops=flops, transcendentals=0, bytes_accessed=flops // 500)


def make_keys(base, rows_dev, ids_ref, key_low, key_high, key_count):
    bag = ids_ref.shape[1]
    own, low, lead = [], [], []
    for j in range(bag):
        ids = ids_ref[:, j, :]
        shifted = ids - base
        good = jnp.logical_and(ids >= 0, jnp.logical_and(shifted >= 0, shifted < rows_dev))
        own.append(jnp.where(good, shifted, -1))
        low.append(shifted & (LOW - 1))
        fresh = good
        for k in range(j):
            fresh = jnp.logical_and(fresh, own[k] != own[j])
        lead.append(fresh)
    deepest = jnp.zeros(own[0].shape, I32)
    for j in range(bag):
        count = jnp.ones(own[0].shape, F32)
        for k in range(j + 1, bag):
            count = count + jnp.where(own[k] == own[j], 1.0, 0.0)
        level = jnp.zeros(own[0].shape, I32)
        for k in range(j):
            level = level + jnp.where(jnp.logical_and(lead[k], low[k] == low[j]), 1, 0)
        key_low[j] = jnp.where(lead[j], low[j] + LOW * level, -1).astype(F32)
        key_high[j] = (own[j] >> (LOW.bit_length() - 1)).astype(F32)
        key_count[j] = count
        deepest = jnp.maximum(deepest, jnp.where(lead[j], level + 1, 0))
    return deepest


def spread(ref, j, source):
    return jnp.broadcast_to(ref[j, pl.ds(source, 1), :], (16, LANES)).astype(BF)


def first_layers(source, key_low, key_high, key_count):
    bag = key_low.shape[0]
    lows = [spread(key_low, j, source) for j in range(bag)]
    highs = [spread(key_high, j, source) for j in range(bag)]
    counts = [spread(key_count, j, source) for j in range(bag)]
    sub = lax.broadcasted_iota(I32, (16, LANES), 0).astype(F32)
    layers = []
    for depth in range(2):
        high_rows, count_rows = [], []
        for group in range(LOW // 16):
            place = (sub + float(LOW * depth + 16 * group)).astype(BF)
            high = jnp.full((16, LANES), -1.0, BF)
            count = jnp.zeros((16, LANES), BF)
            for j in range(bag):
                hit = lows[j] == place
                high = jnp.where(hit, highs[j], high)
                count = jnp.where(hit, counts[j], count)
            high_rows.append(high)
            count_rows.append(count)
        layers.append((jnp.concatenate(high_rows, axis=0), jnp.concatenate(count_rows, axis=0)))
    return layers


def deep_layer(source, depth, key_low, key_high, key_count):
    bag = key_low.shape[0]
    place = (lax.broadcasted_iota(I32, (LOW, LANES), 0) + LOW * depth).astype(F32)
    high = jnp.full((LOW, LANES), -1.0, F32)
    count = jnp.zeros((LOW, LANES), F32)
    for j in range(bag):
        hit = jnp.broadcast_to(key_low[j, pl.ds(source, 1), :], (LOW, LANES)) == place
        high = jnp.where(hit, jnp.broadcast_to(key_high[j, pl.ds(source, 1), :], (LOW, LANES)), high)
        count = jnp.where(hit, jnp.broadcast_to(key_count[j, pl.ds(source, 1), :], (LOW, LANES)), count)
    return high.astype(BF), count.astype(BF)


def counts_for(block, layers):
    want = jnp.asarray(block, F32).astype(BF)
    tile = jnp.zeros((LOW, LANES), BF)
    for high, count in layers:
        tile = jnp.where(high == want, count, tile)
    return tile


def pool_kernel(per_step, base_ref, ids_ref, upper_ref, lower_ref, out_ref, highs_ref, counts_ref, depth_ref,
                key_low, key_high, key_count):
    step = pl.program_id(0)
    width = out_ref.shape[1]
    rows_dev = upper_ref.shape[1]
    sources = ids_ref.shape[0]

    def build(at):
        for s in range(per_step):
            layers = first_layers(at * per_step + s, key_low, key_high, key_count)
            for depth in range(2):
                highs_ref[depth, at * per_step + s] = layers[depth][0]
                counts_ref[depth, at * per_step + s] = layers[depth][1]

    @pl.when(step == 0)
    def _():
        deepest = make_keys(base_ref[0], rows_dev, ids_ref, key_low, key_high, key_count)
        depth_ref[0] = jnp.max(deepest)

        @pl.when(depth_ref[0] > 2)
        def _():
            for s in range(sources):
                depth_ref[1 + s] = jnp.max(deepest[s : s + 1])

        build(0)

    layers = [[(highs_ref[depth, step * per_step + s], counts_ref[depth, step * per_step + s])
               for depth in range(2)] for s in range(per_step)]
    both = lambda cols: jnp.concatenate([upper_ref[:, cols], lower_ref[:, cols]], axis=0)
    chunk = 512
    total = jnp.zeros((2 * width, LANES * per_step), F32)
    for c in range(0, rows_dev, chunk):
        tile = jnp.concatenate(
            [jnp.concatenate([counts_for(c // LOW + h, layers[s]) for h in range(chunk // LOW)], axis=0)
             for s in range(per_step)], axis=1)
        total = total + jnp.dot(both(slice(c, c + chunk)), tile, preferred_element_type=F32)
    for s in range(per_step):
        cols = slice(LANES * s, LANES * (s + 1))
        out_ref[s] = total[0:width, cols] + total[width : 2 * width, cols]

    build(jnp.minimum(step + 1, sources // per_step - 1))

    @pl.when(depth_ref[0] > 2)
    def _():
        for s in range(per_step):
            source = step * per_step + s

            def deeper(depth, carry):
                extra = deep_layer(source, depth, key_low, key_high, key_count)
                wide = 512

                def add(block, value):
                    tile = jnp.concatenate([counts_for(block * (wide // LOW) + h, [extra])
                                            for h in range(wide // LOW)], axis=0)
                    return value + jnp.dot(both(pl.ds(pl.multiple_of(block * wide, wide), wide)),
                                           tile, preferred_element_type=F32)

                more = lax.fori_loop(0, rows_dev // wide, add, jnp.zeros((2 * width, LANES), F32))
                out_ref[s] += more[0:width] + more[width : 2 * width]
                return carry

            lax.fori_loop(2, depth_ref[1 + source], deeper, 0)


def pool(base, ids, parts):
    sources, bag, _ = ids.shape
    width, rows_dev = parts[0].shape
    per_step = 2
    keys = pltpu.VMEM((bag, sources, LANES), F32)
    layer = jax.ShapeDtypeStruct((2, sources, LOW, LANES), BF)
    return pl.pallas_call(
        functools.partial(pool_kernel, per_step),
        grid=(sources // per_step,),
        in_specs=[SCALARS, WHOLE, WHOLE, WHOLE],
        out_specs=[pl.BlockSpec((per_step, width, LANES), lambda i: (i, 0, 0)), WHOLE, WHOLE, SCALARS],
        out_shape=[
            jax.ShapeDtypeStruct((sources, width, LANES), F32),
            layer,
            layer,
            jax.ShapeDtypeStruct((1 + sources,), I32),
        ],
        scratch_shapes=[keys, keys, keys],
        compiler_params=pltpu.CompilerParams(dimension_semantics=("arbitrary",), vmem_limit_bytes=GRANT),
        cost_estimate=estimate(width, rows_dev, sources * LANES),
        name="pool",
    )(base, ids, *parts)


def grad_kernel(blk, steps, rows_dev, base_ref, first_ref, *refs):
    halves = [refs[0:6], refs[6:12]]
    outs, (key_low, key_high, key_count) = refs[12:-3], refs[-3:]
    half = outs[0].shape[0]
    width = 2 * half
    step = pl.program_id(0)
    start = first_ref[step // steps] + step % steps * (blk // LOW)
    together = 4
    total = jnp.zeros((2 * width, blk), F32)
    for ids_ref, upper_ref, lower_ref, highs_ref, counts_ref, depth_ref in halves:
        for s in range(0, ids_ref.shape[0], together):
            tile = jnp.concatenate(
                [jnp.concatenate([counts_for(start + h, [(highs_ref[d, s + t], counts_ref[d, s + t]) for d in range(2)])
                                  for h in range(blk // LOW)], axis=0)
                 for t in range(together)], axis=1)
            lhs = jnp.concatenate([jnp.concatenate([upper_ref[s + t], lower_ref[s + t]], axis=0)
                                   for t in range(together)], axis=1)
            total = total + lax.dot_general(lhs, tile,
                                            (((1,), (1,)), ((), ())), preferred_element_type=F32)

    def put(value, more):
        for group in range(len(outs) // 2):
            @pl.when(step // steps == group)
            def _():
                for ref, at in ((outs[2 * group], 0), (outs[2 * group + 1], half)):
                    new = value[at : at + half] + value[width + at : width + at + half]
                    ref[...] = ref[...] + new if more else new

    put(total, False)

    for ids_ref, upper_ref, lower_ref, highs_ref, counts_ref, depth_ref in halves:
        @pl.when(depth_ref[0] > 2)
        def _():
            make_keys(base_ref[0], rows_dev, ids_ref, key_low, key_high, key_count)

            def visit(s, carry):
                def deeper(depth, inner):
                    extra = deep_layer(s, depth, key_low, key_high, key_count)
                    tile = jnp.concatenate([counts_for(start + h, [extra]) for h in range(blk // LOW)], axis=0)
                    lhs = jnp.concatenate([upper_ref[s], lower_ref[s]], axis=0)
                    more = lax.dot_general(lhs, tile,
                                           (((1,), (1,)), ((), ())), preferred_element_type=F32)
                    put(more, True)
                    return inner

                return lax.fori_loop(2, depth_ref[1 + s], deeper, carry)

            lax.fori_loop(0, ids_ref.shape[0], visit, 0)


def grads(base, firsts, rows, rows_dev, own, other):
    sources, bag, _ = own[0].shape
    width = own[1].shape[1]
    blk = 256
    steps = rows // blk
    keys = pltpu.VMEM((bag, sources, LANES), F32)
    outs = [pl.BlockSpec((width // 2, blk), lambda i, g=g: (0, jnp.clip(i - g * steps, 0, steps - 1)))
            for g in range(len(firsts)) for _ in range(2)]
    each = [WHOLE, WHOLE, WHOLE, WHOLE, WHOLE, SCALARS]
    return pl.pallas_call(
        functools.partial(grad_kernel, blk, steps, rows_dev),
        grid=(steps * len(firsts),),
        in_specs=[SCALARS, SCALARS] + each + each,
        out_specs=outs,
        out_shape=[jax.ShapeDtypeStruct((width // 2, rows), F32)] * len(outs),
        scratch_shapes=[keys, keys, keys],
        compiler_params=pltpu.CompilerParams(dimension_semantics=("arbitrary",), vmem_limit_bytes=GRANT),
        cost_estimate=estimate(width, rows * len(firsts), 2 * sources * LANES),
        name="grads",
    )(base, jnp.stack(firsts).astype(I32) // LOW, *own, *other)


def to_all(x, axis):
    return lax.all_to_all(x, axis, split_axis=0, concat_axis=0, tiled=True)


def shifted(x, axis, by):
    n = lax.axis_size(axis)
    return lax.ppermute(x, axis, [(i, (i + by) % n) for i in range(n)])


def inner(emb_table, feature_ids, lengths, cotangent):
    rows_dev, width = emb_table.shape
    examples, features, bag = feature_ids.shape
    chips = lax.axis_size("x")
    cores = lax.axis_size("core")
    reps = lax.axis_size("rep")
    core = lax.axis_index("core")
    rep = lax.axis_index("rep")
    base = ((lax.axis_index("x") * cores + core) * rows_dev).astype(I32).reshape(1)

    ids_t = jnp.transpose(feature_ids, (1, 2, 0))
    lengths_t = jnp.transpose(lengths, (1, 0))
    share = 1.0 / lengths_t.astype(F32)
    slot = lax.broadcasted_iota(I32, ids_t.shape, 1)
    masked = jnp.where(slot < lengths_t[:, None, :], ids_t, -1)
    spread_ids = jnp.repeat(masked, chips * cores, axis=0)
    ids = to_all(spread_ids, ("z", "x", "core"))
    parts = two_parts(jnp.transpose(emb_table))
    ids = ids.reshape(features * chips, cores, bag, examples)
    ids_own = lax.dynamic_index_in_dim(ids, core, 1, keepdims=False)
    ids_other = lax.dynamic_index_in_dim(ids, 1 - core, 1, keepdims=False)

    scaled = jnp.transpose(cotangent, (1, 2, 0)) * share[:, None, :]
    scaled_own = to_all(jnp.repeat(scaled, chips, axis=0), ("z", "x"))
    scaled_other = shifted(scaled_own, "core", 1)

    sent, *layers_other = pool(base, ids_other, parts)
    sent = shifted(sent, "core", 1)
    kept, *layers_own = pool(base, ids_own, parts)
    pooled = to_all(kept + sent, ("z", "x")).reshape(features, chips, width, examples)
    pooled = jnp.sum(pooled, axis=1) * share[:, None, :]

    own = [ids_own, *two_parts(scaled_own), *layers_own]
    other = [ids_other, *two_parts(scaled_other), *layers_other]
    rows = rows_dev // reps

    def blocks(*ahead):
        return grads(base, [(rep + a) % reps * rows for a in ahead], rows, rows_dev, own, other)

    far_top, far_bottom = blocks(2)
    from_left = shifted(far_top, "rep", 1)
    from_right = shifted(far_bottom, "rep", -1)
    next_top, next_bottom, prev_top, prev_bottom = blocks(1, reps - 1)
    got_bottom = shifted(next_bottom, "rep", 1)
    got_top = shifted(prev_top, "rep", -1)
    got_left_top = shifted(next_top + from_left, "rep", 1)
    got_right_bottom = shifted(prev_bottom + from_right, "rep", -1)
    here_top, here_bottom = blocks(0)
    row_grads = jnp.concatenate(
        [here_top + got_top + got_left_top, here_bottom + got_bottom + got_right_bottom], axis=0
    )
    return jnp.transpose(pooled, (2, 0, 1)), jnp.transpose(row_grads)


def solution(mesh):
    devices = mesh.devices.reshape(4, 4, 2, mesh.shape["rep"])
    fine = Mesh(devices, ("z", "x", "core", "rep"))
    dev = ("z", "x", "core")
    every = ("z", "x", "core", "rep")
    return jax.shard_map(
        inner,
        mesh=fine,
        in_specs=(P(dev, None), P(every, None, None), P(every, None), P(every, None, None)),
        out_specs=(P(every, None, None), P(every, None)),
        check_vma=False,
    )
```

```python
import functools

import jax
import jax.numpy as jnp
from jax import lax
from jax.experimental import pallas as pl
from jax.experimental.pallas import tpu as pltpu
from jax.sharding import Mesh
from jax.sharding import PartitionSpec as P


LOW = 64
CHUNK = 256
TOGETHER = 2
GRANT = 20 * 1024 * 1024
LANES = 128
BF = jnp.bfloat16
F32 = jnp.float32
I32 = jnp.int32
WHOLE = pl.BlockSpec(memory_space=pltpu.VMEM)
SCALARS = pl.BlockSpec(memory_space=pltpu.SMEM)


def two_parts(x):
    high = lax.reduce_precision(x, exponent_bits=8, mantissa_bits=7)
    return high.astype(BF), (x - high).astype(BF)


def estimate(width, rows, columns):
    flops = 4 * width * rows * columns
    return pl.CostEstimate(flops=flops, transcendentals=0, bytes_accessed=flops // 500)


def make_keys(base, rows_dev, ids_ref, key_low, key_high, key_count):
    bag = ids_ref.shape[1]
    own, low, lead = [], [], []
    for j in range(bag):
        ids = ids_ref[:, j, :]
        shifted = ids - base
        good = jnp.logical_and(ids >= 0, jnp.logical_and(shifted >= 0, shifted < rows_dev))
        own.append(jnp.where(good, shifted, -1))
        low.append(shifted & (LOW - 1))
        fresh = good
        for k in range(j):
            fresh = jnp.logical_and(fresh, own[k] != own[j])
        lead.append(fresh)
    deepest = jnp.zeros(own[0].shape, I32)
    for j in range(bag):
        count = jnp.ones(own[0].shape, F32)
        for k in range(j + 1, bag):
            count = count + jnp.where(own[k] == own[j], 1.0, 0.0)
        level = jnp.zeros(own[0].shape, I32)
        for k in range(j):
            level = level + jnp.where(jnp.logical_and(lead[k], low[k] == low[j]), 1, 0)
        key_low[j] = jnp.where(lead[j], low[j] + LOW * level, -1).astype(F32)
        key_high[j] = (own[j] >> (LOW.bit_length() - 1)).astype(F32)
        key_count[j] = count
        deepest = jnp.maximum(deepest, jnp.where(lead[j], level + 1, 0))
    return deepest


def spread(ref, j, source):
    return jnp.broadcast_to(ref[j, pl.ds(source, 1), :], (16, LANES)).astype(BF)


def first_layers(source, key_low, key_high, key_count):
    bag = key_low.shape[0]
    lows = [spread(key_low, j, source) for j in range(bag)]
    highs = [spread(key_high, j, source) for j in range(bag)]
    counts = [spread(key_count, j, source) for j in range(bag)]
    sub = lax.broadcasted_iota(I32, (16, LANES), 0).astype(F32)
    layers = []
    for depth in range(2):
        high_rows, count_rows = [], []
        for group in range(LOW // 16):
            place = (sub + float(LOW * depth + 16 * group)).astype(BF)
            high = jnp.full((16, LANES), -1.0, BF)
            count = jnp.zeros((16, LANES), BF)
            for j in range(bag):
                hit = lows[j] == place
                high = jnp.where(hit, highs[j], high)
                count = jnp.where(hit, counts[j], count)
            high_rows.append(high)
            count_rows.append(count)
        layers.append((jnp.concatenate(high_rows, axis=0), jnp.concatenate(count_rows, axis=0)))
    return layers


def deep_layer(source, depth, key_low, key_high, key_count):
    bag = key_low.shape[0]
    place = (lax.broadcasted_iota(I32, (LOW, LANES), 0) + LOW * depth).astype(F32)
    high = jnp.full((LOW, LANES), -1.0, F32)
    count = jnp.zeros((LOW, LANES), F32)
    for j in range(bag):
        hit = jnp.broadcast_to(key_low[j, pl.ds(source, 1), :], (LOW, LANES)) == place
        high = jnp.where(hit, jnp.broadcast_to(key_high[j, pl.ds(source, 1), :], (LOW, LANES)), high)
        count = jnp.where(hit, jnp.broadcast_to(key_count[j, pl.ds(source, 1), :], (LOW, LANES)), count)
    return high.astype(BF), count.astype(BF)


def counts_for(block, layers):
    want = jnp.asarray(block, F32).astype(BF)
    tile = jnp.zeros((LOW, LANES), BF)
    for high, count in layers:
        tile = jnp.where(high == want, count, tile)
    return tile


def pool_kernel(per_step, base_ref, ids_ref, upper_ref, lower_ref, out_ref, highs_ref, counts_ref, depth_ref,
                key_low, key_high, key_count):
    step = pl.program_id(0)
    width = out_ref.shape[1]
    rows_dev = upper_ref.shape[1]
    sources = ids_ref.shape[0]

    def build(at):
        for s in range(per_step):
            layers = first_layers(at * per_step + s, key_low, key_high, key_count)
            for depth in range(2):
                highs_ref[depth, at * per_step + s] = layers[depth][0]
                counts_ref[depth, at * per_step + s] = layers[depth][1]

    @pl.when(step == 0)
    def _():
        deepest = make_keys(base_ref[0], rows_dev, ids_ref, key_low, key_high, key_count)
        depth_ref[0] = jnp.max(deepest)

        @pl.when(depth_ref[0] > 2)
        def _():
            for s in range(sources):
                depth_ref[1 + s] = jnp.max(deepest[s : s + 1])

        build(0)

    layers = [[(highs_ref[depth, step * per_step + s], counts_ref[depth, step * per_step + s])
               for depth in range(2)] for s in range(per_step)]
    both = lambda cols: jnp.concatenate([upper_ref[:, cols], lower_ref[:, cols]], axis=0)
    chunk = CHUNK
    total = jnp.zeros((2 * width, LANES * per_step), F32)
    for c in range(0, rows_dev, chunk):
        tile = jnp.concatenate(
            [jnp.concatenate([counts_for(c // LOW + h, layers[s]) for h in range(chunk // LOW)], axis=0)
             for s in range(per_step)], axis=1)
        total = total + jnp.dot(both(slice(c, c + chunk)), tile, preferred_element_type=F32)
    for s in range(per_step):
        cols = slice(LANES * s, LANES * (s + 1))
        out_ref[s] = total[0:width, cols] + total[width : 2 * width, cols]

    build(jnp.minimum(step + 1, sources // per_step - 1))

    @pl.when(depth_ref[0] > 2)
    def _():
        for s in range(per_step):
            source = step * per_step + s

            def deeper(depth, carry):
                extra = deep_layer(source, depth, key_low, key_high, key_count)
                wide = 512

                def add(block, value):
                    tile = jnp.concatenate([counts_for(block * (wide // LOW) + h, [extra])
                                            for h in range(wide // LOW)], axis=0)
                    return value + jnp.dot(both(pl.ds(pl.multiple_of(block * wide, wide), wide)),
                                           tile, preferred_element_type=F32)

                more = lax.fori_loop(0, rows_dev // wide, add, jnp.zeros((2 * width, LANES), F32))
                out_ref[s] += more[0:width] + more[width : 2 * width]
                return carry

            lax.fori_loop(2, depth_ref[1 + source], deeper, 0)


def pool(base, ids, parts):
    sources, bag, _ = ids.shape
    width, rows_dev = parts[0].shape
    per_step = 2
    keys = jax.ShapeDtypeStruct((bag, sources, LANES), F32)
    layer = jax.ShapeDtypeStruct((2, sources, LOW, LANES), BF)
    return pl.pallas_call(
        functools.partial(pool_kernel, per_step),
        grid=(sources // per_step,),
        in_specs=[SCALARS, WHOLE, WHOLE, WHOLE],
        out_specs=[pl.BlockSpec((per_step, width, LANES), lambda i: (i, 0, 0)), WHOLE, WHOLE, SCALARS, WHOLE, WHOLE, WHOLE],
        out_shape=[
            jax.ShapeDtypeStruct((sources, width, LANES), F32),
            layer,
            layer,
            jax.ShapeDtypeStruct((1 + sources,), I32),
            keys,
            keys,
            keys,
        ],
        compiler_params=pltpu.CompilerParams(dimension_semantics=("arbitrary",), vmem_limit_bytes=GRANT),
        cost_estimate=estimate(width, rows_dev, sources * LANES),
        name="pool",
    )(base, ids, *parts)


def grad_kernel(blk, steps, first_ref, *refs):
    halves, outs = [refs[0:8], refs[8:16]], refs[16:]
    half = outs[0].shape[0]
    width = 2 * half
    step = pl.program_id(0)
    start = first_ref[step // steps] + step % steps * (blk // LOW)
    together = TOGETHER
    total = jnp.zeros((2 * width, blk), F32)
    for upper_ref, lower_ref, highs_ref, counts_ref, depth_ref, *keys in halves:
        for s in range(0, upper_ref.shape[0], together):
            tile = jnp.concatenate(
                [jnp.concatenate([counts_for(start + h, [(highs_ref[d, s + t], counts_ref[d, s + t]) for d in range(2)])
                                  for h in range(blk // LOW)], axis=0)
                 for t in range(together)], axis=1)
            lhs = jnp.concatenate([jnp.concatenate([upper_ref[s + t], lower_ref[s + t]], axis=0)
                                   for t in range(together)], axis=1)
            total = total + lax.dot_general(lhs, tile,
                                            (((1,), (1,)), ((), ())), preferred_element_type=F32)

    def put(value, more):
        for group in range(len(outs) // 2):
            @pl.when(step // steps == group)
            def _():
                for ref, at in ((outs[2 * group], 0), (outs[2 * group + 1], half)):
                    new = value[at : at + half] + value[width + at : width + at + half]
                    ref[...] = ref[...] + new if more else new

    put(total, False)

    for upper_ref, lower_ref, highs_ref, counts_ref, depth_ref, *keys in halves:
        @pl.when(depth_ref[0] > 2)
        def _():
            def visit(s, carry):
                def deeper(depth, inner):
                    extra = deep_layer(s, depth, *keys)
                    tile = jnp.concatenate([counts_for(start + h, [extra]) for h in range(blk // LOW)], axis=0)
                    lhs = jnp.concatenate([upper_ref[s], lower_ref[s]], axis=0)
                    more = lax.dot_general(lhs, tile,
                                           (((1,), (1,)), ((), ())), preferred_element_type=F32)
                    put(more, True)
                    return inner

                return lax.fori_loop(2, depth_ref[1 + s], deeper, carry)

            lax.fori_loop(0, upper_ref.shape[0], visit, 0)


def grads(firsts, rows, own, other):
    sources, width, _ = own[0].shape
    blk = 256
    steps = rows // blk
    outs = [pl.BlockSpec((width // 2, blk), lambda i, g=g: (0, jnp.clip(i - g * steps, 0, steps - 1)))
            for g in range(len(firsts)) for _ in range(2)]
    each = [WHOLE, WHOLE, WHOLE, WHOLE, SCALARS, WHOLE, WHOLE, WHOLE]
    return pl.pallas_call(
        functools.partial(grad_kernel, blk, steps),
        grid=(steps * len(firsts),),
        in_specs=[SCALARS] + each + each,
        out_specs=outs,
        out_shape=[jax.ShapeDtypeStruct((width // 2, rows), F32)] * len(outs),
        compiler_params=pltpu.CompilerParams(dimension_semantics=("arbitrary",), vmem_limit_bytes=GRANT),
        cost_estimate=estimate(width, rows * len(firsts), 2 * sources * LANES),
        name="grads",
    )(jnp.stack(firsts).astype(I32) // LOW, *own, *other)


def to_all(x, axis):
    return lax.all_to_all(x, axis, split_axis=0, concat_axis=0, tiled=True)


def shifted(x, axis, by):
    n = lax.axis_size(axis)
    return lax.ppermute(x, axis, [(i, (i + by) % n) for i in range(n)])


def inner(emb_table, feature_ids, lengths, cotangent):
    rows_dev, width = emb_table.shape
    examples, features, bag = feature_ids.shape
    chips = lax.axis_size("x")
    cores = lax.axis_size("core")
    reps = lax.axis_size("rep")
    core = lax.axis_index("core")
    rep = lax.axis_index("rep")
    base = ((lax.axis_index("x") * cores + core) * rows_dev).astype(I32).reshape(1)

    ids_t = jnp.transpose(feature_ids, (1, 2, 0))
    lengths_t = jnp.transpose(lengths, (1, 0))
    share = 1.0 / lengths_t.astype(F32)
    slot = lax.broadcasted_iota(I32, ids_t.shape, 1)
    masked = jnp.where(slot < lengths_t[:, None, :], ids_t, -1)
    spread_ids = jnp.repeat(masked, chips * cores, axis=0)
    ids = to_all(spread_ids, ("z", "x", "core"))
    parts = two_parts(jnp.transpose(emb_table))
    ids = ids.reshape(features * chips, cores, bag, examples)
    ids_own = lax.dynamic_index_in_dim(ids, core, 1, keepdims=False)
    ids_other = lax.dynamic_index_in_dim(ids, 1 - core, 1, keepdims=False)

    scaled = jnp.transpose(cotangent, (1, 2, 0)) * share[:, None, :]
    spread_cot = jnp.repeat(scaled, chips, axis=0)
    scaled_own = to_all(spread_cot, ("z", "x"))
    scaled_other = shifted(scaled_own, "core", 1)

    sent, *layers_other = pool(base, ids_other, parts)
    sent = shifted(sent, "core", 1)
    kept, *layers_own = pool(base, ids_own, parts)
    pooled = to_all(kept + sent, ("z", "x")).reshape(features, chips, width, examples)
    pooled = jnp.sum(pooled, axis=1) * share[:, None, :]

    own = [*two_parts(scaled_own), *layers_own]
    other = [*two_parts(scaled_other), *layers_other]
    rows = rows_dev // reps

    def blocks(*ahead):
        return grads([(rep + a) % reps * rows for a in ahead], rows, own, other)

    far_top, far_bottom = blocks(2)
    from_left = shifted(far_top, "rep", 1)
    from_right = shifted(far_bottom, "rep", -1)
    next_top, next_bottom, prev_top, prev_bottom = blocks(1, reps - 1)
    got_bottom = shifted(next_bottom, "rep", 1)
    got_top = shifted(prev_top, "rep", -1)
    got_left_top = shifted(next_top + from_left, "rep", 1)
    got_right_bottom = shifted(prev_bottom + from_right, "rep", -1)
    here_top, here_bottom = blocks(0)
    row_grads = jnp.concatenate(
        [here_top + got_top + got_left_top, here_bottom + got_bottom + got_right_bottom], axis=0
    )
    return jnp.transpose(pooled, (2, 0, 1)), jnp.transpose(row_grads)


def solution(mesh):
    devices = mesh.devices.reshape(4, 4, 2, mesh.shape["rep"])
    fine = Mesh(devices, ("z", "x", "core", "rep"))
    dev = ("z", "x", "core")
    every = ("z", "x", "core", "rep")
    return jax.shard_map(
        inner,
        mesh=fine,
        in_specs=(P(dev, None), P(every, None, None), P(every, None), P(every, None, None)),
        out_specs=(P(every, None, None), P(every, None)),
        check_vma=False,
    )
```

```python
import functools

import jax
import jax.numpy as jnp
from jax import lax
from jax.experimental import pallas as pl
from jax.experimental.pallas import tpu as pltpu
from jax.sharding import Mesh
from jax.sharding import PartitionSpec as P


LOW = 64
DEPTHS = 8
REPS = 4
CHUNK = 256
TOGETHER = 2
GRANT = 20 * 1024 * 1024
SMALL = 8 * 1024 * 1024
LANES = 128
BF = jnp.bfloat16
F32 = jnp.float32
I32 = jnp.int32
WHOLE = pl.BlockSpec(memory_space=pltpu.VMEM)
SCALARS = pl.BlockSpec(memory_space=pltpu.SMEM)


def two_parts(x):
    high = lax.reduce_precision(x, exponent_bits=8, mantissa_bits=7)
    return high.astype(BF), (x - high).astype(BF)


def split_blocks(blocks):
    shape = jax.ShapeDtypeStruct(blocks.shape, BF)

    def kernel(x_ref, upper_ref, lower_ref):
        x = x_ref[...]
        high = x.astype(BF)
        upper_ref[...] = high
        lower_ref[...] = (x - high.astype(F32)).astype(BF)

    part = pl.BlockSpec((4, *blocks.shape[1:]), lambda i: (i, 0, 0))
    return pl.pallas_call(
        kernel,
        grid=(blocks.shape[0] // 4,),
        in_specs=[part],
        out_specs=[part, part],
        out_shape=[shape, shape],
        compiler_params=pltpu.CompilerParams(vmem_limit_bytes=SMALL),
        name="split_blocks",
    )(blocks)


def add_blocks(x, y):
    def kernel(x_ref, y_ref, out_ref):
        out_ref[...] = x_ref[...] + y_ref[...]

    part = pl.BlockSpec((4, *x.shape[1:]), lambda i: (i, 0, 0))
    return pl.pallas_call(
        kernel,
        grid=(x.shape[0] // 4,),
        in_specs=[part, part],
        out_specs=part,
        out_shape=jax.ShapeDtypeStruct(x.shape, F32),
        compiler_params=pltpu.CompilerParams(vmem_limit_bytes=SMALL),
        name="add_blocks",
    )(x, y)


def finish_pool(sums, lengths_t):
    features, chips, width, lanes = sums.shape

    def kernel(x_ref, lengths_ref, out_ref):
        share = 1.0 / lengths_ref[pl.ds(pl.program_id(0), 1), :].astype(F32)
        total = x_ref[0]
        for chip in range(1, chips):
            total = total + x_ref[chip]
        out_ref[...] = total * share

    return pl.pallas_call(
        kernel,
        grid=(features,),
        in_specs=[
            pl.BlockSpec((None, chips, width, lanes), lambda i: (i, 0, 0, 0)),
            pl.BlockSpec((features, lanes), lambda i: (0, 0)),
        ],
        out_specs=pl.BlockSpec((None, width, lanes), lambda i: (i, 0, 0)),
        out_shape=jax.ShapeDtypeStruct((features, width, lanes), F32),
        compiler_params=pltpu.CompilerParams(vmem_limit_bytes=SMALL),
        name="finish_pool",
    )(sums, lengths_t)


def add_into(block, piece, at):
    def kernel(block_ref, piece_ref, out_ref):
        size = piece_ref.shape[0]
        other = size if at == 0 else 0
        out_ref[at : at + size] = block_ref[at : at + size] + piece_ref[...]
        out_ref[other : other + size] = block_ref[other : other + size]

    cols = block.shape[1] // 2
    spec = lambda x: pl.BlockSpec((x.shape[0], cols), lambda i: (0, i))
    return pl.pallas_call(
        kernel,
        grid=(2,),
        in_specs=[spec(block), spec(piece)],
        out_specs=spec(block),
        out_shape=jax.ShapeDtypeStruct(block.shape, F32),
        compiler_params=pltpu.CompilerParams(vmem_limit_bytes=SMALL),
        name="add_into",
    )(block, piece)


def estimate(width, rows, columns):
    flops = 4 * width * rows * columns
    return pl.CostEstimate(flops=flops, transcendentals=0, bytes_accessed=flops // 500)


def make_keys(base, rows_dev, ids_ref, key_low, key_high, key_count):
    bag = ids_ref.shape[1]
    own, low, lead = [], [], []
    for j in range(bag):
        ids = ids_ref[:, j, :]
        shifted = ids - base
        good = jnp.logical_and(ids >= 0, jnp.logical_and(shifted >= 0, shifted < rows_dev))
        own.append(jnp.where(good, shifted, -1))
        low.append(shifted & (LOW - 1))
        fresh = good
        for k in range(j):
            fresh = jnp.logical_and(fresh, own[k] != own[j])
        lead.append(fresh)
    deepest = jnp.zeros(own[0].shape, I32)
    for j in range(bag):
        count = jnp.ones(own[0].shape, F32)
        for k in range(j + 1, bag):
            count = count + jnp.where(own[k] == own[j], 1.0, 0.0)
        level = jnp.zeros(own[0].shape, I32)
        for k in range(j):
            level = level + jnp.where(jnp.logical_and(lead[k], low[k] == low[j]), 1, 0)
        key_low[j] = jnp.where(lead[j], low[j] + LOW * level, -1).astype(F32)
        key_high[j] = (own[j] >> (LOW.bit_length() - 1)).astype(F32)
        key_count[j] = count
        deepest = jnp.maximum(deepest, jnp.where(lead[j], level + 1, 0))
    return deepest


def spread(ref, j, source):
    return jnp.broadcast_to(ref[j, pl.ds(source, 1), :], (16, LANES)).astype(BF)


def first_layers(source, key_low, key_high, key_count):
    bag = key_low.shape[0]
    lows = [spread(key_low, j, source) for j in range(bag)]
    highs = [spread(key_high, j, source) for j in range(bag)]
    counts = [spread(key_count, j, source) for j in range(bag)]
    sub = lax.broadcasted_iota(I32, (16, LANES), 0).astype(F32)
    layers = []
    for depth in range(2):
        high_rows, count_rows = [], []
        for group in range(LOW // 16):
            place = (sub + float(LOW * depth + 16 * group)).astype(BF)
            high = jnp.full((16, LANES), -1.0, BF)
            count = jnp.zeros((16, LANES), BF)
            for j in range(bag):
                hit = lows[j] == place
                high = jnp.where(hit, highs[j], high)
                count = jnp.where(hit, counts[j], count)
            high_rows.append(high)
            count_rows.append(count)
        layers.append((jnp.concatenate(high_rows, axis=0), jnp.concatenate(count_rows, axis=0)))
    return layers


def deep_layer(source, depth, key_low, key_high, key_count):
    bag = key_low.shape[0]
    place = (lax.broadcasted_iota(I32, (LOW, LANES), 0) + LOW * depth).astype(F32)
    high = jnp.full((LOW, LANES), -1.0, F32)
    count = jnp.zeros((LOW, LANES), F32)
    for j in range(bag):
        hit = jnp.broadcast_to(key_low[j, pl.ds(source, 1), :], (LOW, LANES)) == place
        high = jnp.where(hit, jnp.broadcast_to(key_high[j, pl.ds(source, 1), :], (LOW, LANES)), high)
        count = jnp.where(hit, jnp.broadcast_to(key_count[j, pl.ds(source, 1), :], (LOW, LANES)), count)
    return high.astype(BF), count.astype(BF)


def counts_for(block, layers):
    want = jnp.asarray(block, F32).astype(BF)
    tile = jnp.zeros((LOW, LANES), BF)
    for high, count in layers:
        tile = jnp.where(high == want, count, tile)
    return tile


def pool_kernel(per_step, base_ref, ids_ref, upper_ref, lower_ref, out_ref, highs_ref, counts_ref, deep_ref,
                key_low, key_high, key_count, next_highs, next_counts):
    step = pl.program_id(0)
    width = out_ref.shape[1]
    rows_dev = upper_ref.shape[1]
    sources = ids_ref.shape[0]

    def build(at):
        for s in range(per_step):
            layers = first_layers(at * per_step + s, key_low, key_high, key_count)
            for depth in range(2):
                next_highs[depth, s] = layers[depth][0]
                next_counts[depth, s] = layers[depth][1]

    @pl.when(step == 0)
    def _():
        deepest = make_keys(base_ref[0], rows_dev, ids_ref, key_low, key_high, key_count)
        deep_ref[0] = 0

        @pl.when(jnp.max(deepest) > 2)
        def _():
            for s in range(sources):
                def note(depth, carry, s=s):
                    deep_ref[0] += 1
                    deep_ref[deep_ref[0]] = s * DEPTHS + depth
                    return carry

                lax.fori_loop(2, jnp.max(deepest[s : s + 1]), note, 0)

        build(0)

    layers = [[(next_highs[depth, s], next_counts[depth, s]) for depth in range(2)] for s in range(per_step)]
    for s in range(per_step):
        for depth in range(2):
            highs_ref[depth, s] = layers[s][depth][0]
            counts_ref[depth, s] = layers[s][depth][1]
    both = lambda cols: jnp.concatenate([upper_ref[:, cols], lower_ref[:, cols]], axis=0)
    chunk = CHUNK
    total = jnp.zeros((2 * width, LANES * per_step), F32)
    for c in range(0, rows_dev, chunk):
        tile = jnp.concatenate(
            [jnp.concatenate([counts_for(c // LOW + h, layers[s]) for h in range(chunk // LOW)], axis=0)
             for s in range(per_step)], axis=1)
        total = total + jnp.dot(both(slice(c, c + chunk)), tile, preferred_element_type=F32)
    for s in range(per_step):
        cols = slice(LANES * s, LANES * (s + 1))
        out_ref[s] = total[0:width, cols] + total[width : 2 * width, cols]

    build(jnp.minimum(step + 1, sources // per_step - 1))

    def deeper(entry, carry):
        source = deep_ref[1 + entry] // DEPTHS

        @pl.when(source // per_step == step)
        def _():
            extra = deep_layer(source, deep_ref[1 + entry] % DEPTHS, key_low, key_high, key_count)
            wide = 512

            def add(block, value):
                tile = jnp.concatenate([counts_for(block * (wide // LOW) + h, [extra])
                                        for h in range(wide // LOW)], axis=0)
                return value + jnp.dot(both(pl.ds(pl.multiple_of(block * wide, wide), wide)),
                                       tile, preferred_element_type=F32)

            more = lax.fori_loop(0, rows_dev // wide, add, jnp.zeros((2 * width, LANES), F32))
            out_ref[source % per_step] += more[0:width] + more[width : 2 * width]

        return carry

    lax.fori_loop(0, deep_ref[0], deeper, 0)


def pool(base, ids, parts):
    sources, bag, _ = ids.shape
    width, rows_dev = parts[0].shape
    per_step = 2
    keys = jax.ShapeDtypeStruct((bag, sources, LANES), F32)
    layer = jax.ShapeDtypeStruct((2, sources, LOW, LANES), BF)
    shown = pl.BlockSpec((2, per_step, LOW, LANES), lambda i: (0, i, 0, 0))
    staged = pltpu.VMEM((2, per_step, LOW, LANES), BF)
    return pl.pallas_call(
        functools.partial(pool_kernel, per_step),
        grid=(sources // per_step,),
        in_specs=[SCALARS, WHOLE, WHOLE, WHOLE],
        out_specs=[pl.BlockSpec((per_step, width, LANES), lambda i: (i, 0, 0)), shown, shown, SCALARS, WHOLE, WHOLE, WHOLE],
        out_shape=[
            jax.ShapeDtypeStruct((sources, width, LANES), F32),
            layer,
            layer,
            jax.ShapeDtypeStruct((1 + sources * DEPTHS,), I32),
            keys,
            keys,
            keys,
        ],
        scratch_shapes=[staged, staged],
        compiler_params=pltpu.CompilerParams(dimension_semantics=("arbitrary",), vmem_limit_bytes=GRANT),
        cost_estimate=estimate(width, rows_dev, sources * LANES),
        name="pool",
    )(base, ids, *parts)


def grad_kernel(blk, steps, aheads, rep_ref, *refs):
    halves, outs = [refs[0:8], refs[8:16]], refs[16:]
    width = halves[0][0].shape[1]
    step = pl.program_id(0)
    groups = len(aheads)
    ahead = jnp.where(step < steps, aheads[0], aheads[-1])
    start = ((rep_ref[0] + ahead) & (REPS - 1)) * (steps * blk // LOW) + step % steps * (blk // LOW)
    together = TOGETHER
    total = jnp.zeros((2 * width, blk), F32)
    for upper_ref, lower_ref, highs_ref, counts_ref, deep_ref, *keys in halves:
        for s in range(0, upper_ref.shape[0], together):
            tile = jnp.concatenate(
                [jnp.concatenate([counts_for(start + h, [(highs_ref[d, s + t], counts_ref[d, s + t]) for d in range(2)])
                                  for h in range(blk // LOW)], axis=0)
                 for t in range(together)], axis=1)
            lhs = jnp.concatenate([jnp.concatenate([upper_ref[s + t], lower_ref[s + t]], axis=0)
                                   for t in range(together)], axis=1)
            total = total + lax.dot_general(lhs, tile,
                                            (((1,), (1,)), ((), ())), preferred_element_type=F32)

    def put(value, more):
        each = len(outs) // groups
        for group in range(groups):
            @pl.when(step // steps == group)
            def _():
                for part in range(each):
                    ref, at = outs[each * group + part], part * (width // each)
                    new = value[at : at + width // each] + value[width + at : width + at + width // each]
                    ref[...] = ref[...] + new if more else new

    put(total, False)

    for upper_ref, lower_ref, highs_ref, counts_ref, deep_ref, *keys in halves:
        def deeper(entry, carry, upper_ref=upper_ref, lower_ref=lower_ref, deep_ref=deep_ref, keys=keys):
            s = deep_ref[1 + entry] // DEPTHS
            extra = deep_layer(s, deep_ref[1 + entry] % DEPTHS, *keys)
            tile = jnp.concatenate([counts_for(start + h, [extra]) for h in range(blk // LOW)], axis=0)
            lhs = jnp.concatenate([upper_ref[s], lower_ref[s]], axis=0)
            put(lax.dot_general(lhs, tile, (((1,), (1,)), ((), ())), preferred_element_type=F32), True)
            return carry

        lax.fori_loop(0, deep_ref[0], deeper, 0)


def grads(rep, aheads, each, rows, own, other):
    sources, width, _ = own[0].shape
    blk = 256
    steps = rows // blk
    outs = [pl.BlockSpec((width // each, blk), lambda i, g=g: (0, jnp.clip(i - g * steps, 0, steps - 1)))
            for g in range(len(aheads)) for _ in range(each)]
    side = [WHOLE, WHOLE, WHOLE, WHOLE, SCALARS, WHOLE, WHOLE, WHOLE]
    return pl.pallas_call(
        functools.partial(grad_kernel, blk, steps, aheads),
        grid=(steps * len(aheads),),
        in_specs=[SCALARS] + side + side,
        out_specs=outs,
        out_shape=[jax.ShapeDtypeStruct((width // each, rows), F32)] * len(outs),
        compiler_params=pltpu.CompilerParams(dimension_semantics=("arbitrary",), vmem_limit_bytes=GRANT),
        cost_estimate=estimate(width, rows * len(aheads), 2 * sources * LANES),
        name="grads",
    )(rep, *own, *other)


def to_all(x, axis):
    return lax.all_to_all(x, axis, split_axis=0, concat_axis=0, tiled=True)


def shifted(x, axis, by):
    n = lax.axis_size(axis)
    return lax.ppermute(x, axis, [(i, (i + by) % n) for i in range(n)])


def inner(emb_table, feature_ids, lengths, cotangent):
    rows_dev, width = emb_table.shape
    examples, features, bag = feature_ids.shape
    chips = lax.axis_size("x")
    cores = lax.axis_size("core")
    reps = lax.axis_size("rep")
    core = lax.axis_index("core")
    rep = lax.axis_index("rep")
    base = ((lax.axis_index("x") * cores + core) * rows_dev).astype(I32).reshape(1)

    ids_t = jnp.transpose(feature_ids, (1, 2, 0))
    lengths_t = jnp.transpose(lengths, (1, 0))
    share = 1.0 / lengths_t.astype(F32)
    slot = lax.broadcasted_iota(I32, ids_t.shape, 1)
    masked = jnp.where(slot < lengths_t[:, None, :], ids_t, -1)
    spread_ids = jnp.repeat(masked, chips * cores, axis=0)
    ids = to_all(spread_ids, ("z", "x", "core"))
    parts = two_parts(jnp.transpose(emb_table))
    ids = ids.reshape(features * chips, cores, bag, examples)
    ids_own = lax.dynamic_index_in_dim(ids, core, 1, keepdims=False)
    ids_other = lax.dynamic_index_in_dim(ids, 1 - core, 1, keepdims=False)

    scaled = jnp.transpose(cotangent, (1, 2, 0)) * share[:, None, :]
    spread_cot = jnp.broadcast_to(scaled[:, None], (features, chips, width, examples))
    spread_cot = spread_cot.reshape(features * chips, width, examples)
    scaled_own = to_all(spread_cot, ("z", "x"))
    scaled_other = shifted(scaled_own, "core", 1)

    sent, *layers_other = pool(base, ids_other, parts)
    sent = shifted(sent, "core", 1)
    kept, *layers_own = pool(base, ids_own, parts)
    pooled = to_all(add_blocks(kept, sent), ("z", "x")).reshape(features, chips, width, examples)
    pooled = finish_pool(pooled, lengths_t)

    own = [*split_blocks(scaled_own), *layers_own]
    other = [*split_blocks(scaled_other), *layers_other]
    rows = rows_dev // reps

    def blocks(each, *ahead):
        return grads(rep.astype(I32).reshape(1), ahead, each, rows, own, other)

    half = width // 2
    far_top, far_bottom = blocks(2, 2)
    from_left = shifted(far_top, "rep", 1)
    from_right = shifted(far_bottom, "rep", -1)
    ahead, behind = blocks(1, 1, reps - 1)
    ahead = add_into(ahead, from_left, 0)
    behind = add_into(behind, from_right, half)
    got_left = shifted(ahead, "rep", 1)
    got_right = shifted(behind, "rep", -1)
    (here,) = blocks(1, 0)
    row_grads = here + got_left + got_right
    return jnp.transpose(pooled, (2, 0, 1)), jnp.transpose(row_grads)


def solution(mesh):
    devices = mesh.devices.reshape(4, 4, 2, mesh.shape["rep"])
    fine = Mesh(devices, ("z", "x", "core", "rep"))
    dev = ("z", "x", "core")
    every = ("z", "x", "core", "rep")
    return jax.shard_map(
        inner,
        mesh=fine,
        in_specs=(P(dev, None), P(every, None, None), P(every, None), P(every, None, None)),
        out_specs=(P(every, None, None), P(every, None)),
        check_vma=False,
    )
```

```python
import functools

import jax
import jax.numpy as jnp
from jax import lax
from jax.experimental import pallas as pl
from jax.experimental.pallas import tpu as pltpu
from jax.sharding import Mesh
from jax.sharding import PartitionSpec as P


LOW = 64
DEPTHS = 8
REPS = 4
SMALL = 8 * 1024 * 1024
CHUNK = 256
TOGETHER = 2
GRANT = 20 * 1024 * 1024
LANES = 128
BF = jnp.bfloat16
F32 = jnp.float32
I32 = jnp.int32
WHOLE = pl.BlockSpec(memory_space=pltpu.VMEM)
SCALARS = pl.BlockSpec(memory_space=pltpu.SMEM)


def two_parts(x):
    high = lax.reduce_precision(x, exponent_bits=8, mantissa_bits=7)
    return high.astype(BF), (x - high).astype(BF)


def finish_pool(sums, lengths_t):
    features, chips, width, lanes = sums.shape

    def kernel(x_ref, lengths_ref, out_ref):
        share = 1.0 / lengths_ref[pl.ds(pl.program_id(0), 1), :].astype(F32)
        total = x_ref[0]
        for chip in range(1, chips):
            total = total + x_ref[chip]
        out_ref[...] = total * share

    return pl.pallas_call(
        kernel,
        grid=(features,),
        in_specs=[
            pl.BlockSpec((None, chips, width, lanes), lambda i: (i, 0, 0, 0)),
            pl.BlockSpec((features, lanes), lambda i: (0, 0)),
        ],
        out_specs=pl.BlockSpec((None, width, lanes), lambda i: (i, 0, 0)),
        out_shape=jax.ShapeDtypeStruct((features, width, lanes), F32),
        compiler_params=pltpu.CompilerParams(vmem_limit_bytes=SMALL),
        name="finish_pool",
    )(sums, lengths_t)


def join(tops, bottoms):
    half, rows = tops[0].shape
    cols = rows // 2

    def kernel(*refs):
        out_ref = refs[-1]
        out_ref[0:half] = refs[0][...] + refs[1][...] + refs[2][...]
        out_ref[half:] = refs[3][...] + refs[4][...] + refs[5][...]

    spec = lambda n: pl.BlockSpec((n, cols), lambda i: (0, i))
    return pl.pallas_call(
        kernel,
        grid=(2,),
        in_specs=[spec(half)] * 6,
        out_specs=spec(2 * half),
        out_shape=jax.ShapeDtypeStruct((2 * half, rows), F32),
        compiler_params=pltpu.CompilerParams(vmem_limit_bytes=SMALL),
        name="join",
    )(*tops, *bottoms)


def estimate(width, rows, columns):
    flops = 4 * width * rows * columns
    return pl.CostEstimate(flops=flops, transcendentals=0, bytes_accessed=flops // 500)


def make_keys(base, rows_dev, ids_ref, key_low, key_high, key_count):
    bag = ids_ref.shape[1]
    own, low, lead = [], [], []
    for j in range(bag):
        ids = ids_ref[:, j, :]
        shifted = ids - base
        good = jnp.logical_and(ids >= 0, jnp.logical_and(shifted >= 0, shifted < rows_dev))
        own.append(jnp.where(good, shifted, -1))
        low.append(shifted & (LOW - 1))
        fresh = good
        for k in range(j):
            fresh = jnp.logical_and(fresh, own[k] != own[j])
        lead.append(fresh)
    deepest = jnp.zeros(own[0].shape, I32)
    for j in range(bag):
        count = jnp.ones(own[0].shape, F32)
        for k in range(j + 1, bag):
            count = count + jnp.where(own[k] == own[j], 1.0, 0.0)
        level = jnp.zeros(own[0].shape, I32)
        for k in range(j):
            level = level + jnp.where(jnp.logical_and(lead[k], low[k] == low[j]), 1, 0)
        key_low[j] = jnp.where(lead[j], low[j] + LOW * level, -1).astype(F32)
        key_high[j] = (own[j] >> (LOW.bit_length() - 1)).astype(F32)
        key_count[j] = count
        deepest = jnp.maximum(deepest, jnp.where(lead[j], level + 1, 0))
    return deepest


def spread(ref, j, source):
    return jnp.broadcast_to(ref[j, pl.ds(source, 1), :], (16, LANES)).astype(BF)


def first_layers(source, key_low, key_high, key_count):
    bag = key_low.shape[0]
    lows = [spread(key_low, j, source) for j in range(bag)]
    highs = [spread(key_high, j, source) for j in range(bag)]
    counts = [spread(key_count, j, source) for j in range(bag)]
    sub = lax.broadcasted_iota(I32, (16, LANES), 0).astype(F32)
    layers = []
    for depth in range(2):
        high_rows, count_rows = [], []
        for group in range(LOW // 16):
            place = (sub + float(LOW * depth + 16 * group)).astype(BF)
            high = jnp.full((16, LANES), -1.0, BF)
            count = jnp.zeros((16, LANES), BF)
            for j in range(bag):
                hit = lows[j] == place
                high = jnp.where(hit, highs[j], high)
                count = jnp.where(hit, counts[j], count)
            high_rows.append(high)
            count_rows.append(count)
        layers.append((jnp.concatenate(high_rows, axis=0), jnp.concatenate(count_rows, axis=0)))
    return layers


def deep_layer(source, depth, key_low, key_high, key_count):
    bag = key_low.shape[0]
    place = (lax.broadcasted_iota(I32, (LOW, LANES), 0) + LOW * depth).astype(F32)
    high = jnp.full((LOW, LANES), -1.0, F32)
    count = jnp.zeros((LOW, LANES), F32)
    for j in range(bag):
        hit = jnp.broadcast_to(key_low[j, pl.ds(source, 1), :], (LOW, LANES)) == place
        high = jnp.where(hit, jnp.broadcast_to(key_high[j, pl.ds(source, 1), :], (LOW, LANES)), high)
        count = jnp.where(hit, jnp.broadcast_to(key_count[j, pl.ds(source, 1), :], (LOW, LANES)), count)
    return high.astype(BF), count.astype(BF)


def counts_for(block, layers):
    want = jnp.asarray(block, F32).astype(BF)
    tile = jnp.zeros((LOW, LANES), BF)
    for high, count in layers:
        tile = jnp.where(high == want, count, tile)
    return tile


def pool_kernel(per_step, base_ref, ids_ref, upper_ref, lower_ref, out_ref, highs_ref, counts_ref, deep_ref,
                key_low, key_high, key_count):
    step = pl.program_id(0)
    width = out_ref.shape[1]
    rows_dev = upper_ref.shape[1]
    sources = ids_ref.shape[0]

    def build(at):
        for s in range(per_step):
            layers = first_layers(at * per_step + s, key_low, key_high, key_count)
            for depth in range(2):
                highs_ref[depth, at * per_step + s] = layers[depth][0]
                counts_ref[depth, at * per_step + s] = layers[depth][1]

    @pl.when(step == 0)
    def _():
        deepest = make_keys(base_ref[0], rows_dev, ids_ref, key_low, key_high, key_count)
        deep_ref[0] = 0

        @pl.when(jnp.max(deepest) > 2)
        def _():
            for s in range(sources):
                def note(depth, carry, s=s):
                    deep_ref[0] += 1
                    deep_ref[deep_ref[0]] = s * DEPTHS + depth
                    return carry

                lax.fori_loop(2, jnp.max(deepest[s : s + 1]), note, 0)

        build(0)

    layers = [[(highs_ref[depth, step * per_step + s], counts_ref[depth, step * per_step + s])
               for depth in range(2)] for s in range(per_step)]
    both = lambda cols: jnp.concatenate([upper_ref[:, cols], lower_ref[:, cols]], axis=0)
    chunk = CHUNK
    total = jnp.zeros((2 * width, LANES * per_step), F32)
    for c in range(0, rows_dev, chunk):
        tile = jnp.concatenate(
            [jnp.concatenate([counts_for(c // LOW + h, layers[s]) for h in range(chunk // LOW)], axis=0)
             for s in range(per_step)], axis=1)
        total = total + jnp.dot(both(slice(c, c + chunk)), tile, preferred_element_type=F32)
    for s in range(per_step):
        cols = slice(LANES * s, LANES * (s + 1))
        out_ref[s] = total[0:width, cols] + total[width : 2 * width, cols]

    build(jnp.minimum(step + 1, sources // per_step - 1))

    def deeper(entry, carry):
        source = deep_ref[1 + entry] // DEPTHS

        @pl.when(source // per_step == step)
        def _():
            extra = deep_layer(source, deep_ref[1 + entry] % DEPTHS, key_low, key_high, key_count)
            wide = 512

            def add(block, value):
                tile = jnp.concatenate([counts_for(block * (wide // LOW) + h, [extra])
                                        for h in range(wide // LOW)], axis=0)
                return value + jnp.dot(both(pl.ds(pl.multiple_of(block * wide, wide), wide)),
                                       tile, preferred_element_type=F32)

            more = lax.fori_loop(0, rows_dev // wide, add, jnp.zeros((2 * width, LANES), F32))
            out_ref[source % per_step] += more[0:width] + more[width : 2 * width]

        return carry

    lax.fori_loop(0, deep_ref[0], deeper, 0)


def pool(base, ids, parts):
    sources, bag, _ = ids.shape
    width, rows_dev = parts[0].shape
    per_step = 2
    keys = jax.ShapeDtypeStruct((bag, sources, LANES), F32)
    layer = jax.ShapeDtypeStruct((2, sources, LOW, LANES), BF)
    return pl.pallas_call(
        functools.partial(pool_kernel, per_step),
        grid=(sources // per_step,),
        in_specs=[SCALARS, WHOLE, WHOLE, WHOLE],
        out_specs=[pl.BlockSpec((per_step, width, LANES), lambda i: (i, 0, 0)), WHOLE, WHOLE, SCALARS, WHOLE, WHOLE, WHOLE],
        out_shape=[
            jax.ShapeDtypeStruct((sources, width, LANES), F32),
            layer,
            layer,
            jax.ShapeDtypeStruct((1 + sources * DEPTHS,), I32),
            keys,
            keys,
            keys,
        ],
        compiler_params=pltpu.CompilerParams(dimension_semantics=("arbitrary",), vmem_limit_bytes=GRANT),
        cost_estimate=estimate(width, rows_dev, sources * LANES),
        name="pool",
    )(base, ids, *parts)


def grad_kernel(blk, steps, aheads, rep_ref, *refs):
    halves, outs = [refs[0:8], refs[8:16]], refs[16:]
    width = halves[0][0].shape[1]
    step = pl.program_id(0)
    groups = len(aheads)
    ahead = jnp.where(step < steps, aheads[0], aheads[-1])
    start = ((rep_ref[0] + ahead) & (REPS - 1)) * (steps * blk // LOW) + step % steps * (blk // LOW)
    together = TOGETHER
    total = jnp.zeros((2 * width, blk), F32)
    for upper_ref, lower_ref, highs_ref, counts_ref, deep_ref, *keys in halves:
        for s in range(0, upper_ref.shape[0], together):
            tile = jnp.concatenate(
                [jnp.concatenate([counts_for(start + h, [(highs_ref[d, s + t], counts_ref[d, s + t]) for d in range(2)])
                                  for h in range(blk // LOW)], axis=0)
                 for t in range(together)], axis=1)
            lhs = jnp.concatenate([jnp.concatenate([upper_ref[s + t], lower_ref[s + t]], axis=0)
                                   for t in range(together)], axis=1)
            total = total + lax.dot_general(lhs, tile,
                                            (((1,), (1,)), ((), ())), preferred_element_type=F32)

    def put(value, more):
        each = len(outs) // groups
        for group in range(groups):
            @pl.when(step // steps == group)
            def _():
                for part in range(each):
                    ref, at = outs[each * group + part], part * (width // each)
                    new = value[at : at + width // each] + value[width + at : width + at + width // each]
                    ref[...] = ref[...] + new if more else new

    put(total, False)

    for upper_ref, lower_ref, highs_ref, counts_ref, deep_ref, *keys in halves:
        def deeper(entry, carry, upper_ref=upper_ref, lower_ref=lower_ref, deep_ref=deep_ref, keys=keys):
            s = deep_ref[1 + entry] // DEPTHS
            extra = deep_layer(s, deep_ref[1 + entry] % DEPTHS, *keys)
            tile = jnp.concatenate([counts_for(start + h, [extra]) for h in range(blk // LOW)], axis=0)
            lhs = jnp.concatenate([upper_ref[s], lower_ref[s]], axis=0)
            put(lax.dot_general(lhs, tile, (((1,), (1,)), ((), ())), preferred_element_type=F32), True)
            return carry

        lax.fori_loop(0, deep_ref[0], deeper, 0)


def grads(rep, aheads, each, rows, own, other):
    sources, width, _ = own[0].shape
    blk = 256
    steps = rows // blk
    outs = [pl.BlockSpec((width // each, blk), lambda i, g=g: (0, jnp.clip(i - g * steps, 0, steps - 1)))
            for g in range(len(aheads)) for _ in range(each)]
    side = [WHOLE, WHOLE, WHOLE, WHOLE, SCALARS, WHOLE, WHOLE, WHOLE]
    return pl.pallas_call(
        functools.partial(grad_kernel, blk, steps, aheads),
        grid=(steps * len(aheads),),
        in_specs=[SCALARS] + side + side,
        out_specs=outs,
        out_shape=[jax.ShapeDtypeStruct((width // each, rows), F32)] * len(outs),
        compiler_params=pltpu.CompilerParams(dimension_semantics=("arbitrary",), vmem_limit_bytes=GRANT),
        cost_estimate=estimate(width, rows * len(aheads), 2 * sources * LANES),
        name="grads",
    )(rep, *own, *other)


def to_all(x, axis):
    return lax.all_to_all(x, axis, split_axis=0, concat_axis=0, tiled=True)


def shifted(x, axis, by):
    n = lax.axis_size(axis)
    return lax.ppermute(x, axis, [(i, (i + by) % n) for i in range(n)])


def inner(emb_table, feature_ids, lengths, cotangent):
    rows_dev, width = emb_table.shape
    examples, features, bag = feature_ids.shape
    chips = lax.axis_size("x")
    cores = lax.axis_size("core")
    reps = lax.axis_size("rep")
    core = lax.axis_index("core")
    rep = lax.axis_index("rep")
    base = ((lax.axis_index("x") * cores + core) * rows_dev).astype(I32).reshape(1)

    ids_t = jnp.transpose(feature_ids, (1, 2, 0))
    lengths_t = jnp.transpose(lengths, (1, 0))
    share = 1.0 / lengths_t.astype(F32)
    slot = lax.broadcasted_iota(I32, ids_t.shape, 1)
    masked = jnp.where(slot < lengths_t[:, None, :], ids_t, -1)
    spread_ids = jnp.repeat(masked, chips * cores, axis=0)
    ids = to_all(spread_ids, ("z", "x", "core"))
    parts = two_parts(jnp.transpose(emb_table))
    ids = ids.reshape(features * chips, cores, bag, examples)
    ids_own = lax.dynamic_index_in_dim(ids, core, 1, keepdims=False)
    ids_other = lax.dynamic_index_in_dim(ids, 1 - core, 1, keepdims=False)

    scaled = jnp.transpose(cotangent, (1, 2, 0)) * share[:, None, :]
    spread_cot = jnp.broadcast_to(scaled[:, None], (features, chips, width, examples))
    spread_cot = spread_cot.reshape(features * chips, width, examples)
    scaled_own = to_all(spread_cot, ("z", "x"))
    scaled_other = shifted(scaled_own, "core", 1)

    sent, *layers_other = pool(base, ids_other, parts)
    sent = shifted(sent, "core", 1)
    kept, *layers_own = pool(base, ids_own, parts)
    pooled = to_all(kept + sent, ("z", "x")).reshape(features, chips, width, examples)
    pooled = finish_pool(pooled, lengths_t)

    own = [*two_parts(scaled_own), *layers_own]
    other = [*two_parts(scaled_other), *layers_other]
    rows = rows_dev // reps

    def blocks(*ahead):
        return grads(rep.astype(I32).reshape(1), ahead, 2, rows, own, other)

    far_top, far_bottom = blocks(2)
    from_left = shifted(far_top, "rep", 1)
    from_right = shifted(far_bottom, "rep", -1)
    next_top, next_bottom, prev_top, prev_bottom = blocks(1, reps - 1)
    got_bottom = shifted(next_bottom, "rep", 1)
    got_top = shifted(prev_top, "rep", -1)
    got_left_top = shifted(next_top + from_left, "rep", 1)
    got_right_bottom = shifted(prev_bottom + from_right, "rep", -1)
    here_top, here_bottom = blocks(0)
    row_grads = join([here_top, got_top, got_left_top], [here_bottom, got_bottom, got_right_bottom])
    return jnp.transpose(pooled, (2, 0, 1)), jnp.transpose(row_grads)


def solution(mesh):
    devices = mesh.devices.reshape(4, 4, 2, mesh.shape["rep"])
    fine = Mesh(devices, ("z", "x", "core", "rep"))
    dev = ("z", "x", "core")
    every = ("z", "x", "core", "rep")
    return jax.shard_map(
        inner,
        mesh=fine,
        in_specs=(P(dev, None), P(every, None, None), P(every, None), P(every, None, None)),
        out_specs=(P(every, None, None), P(every, None)),
        check_vma=False,
    )
```

```python
import functools

import jax
import jax.numpy as jnp
from jax import lax
from jax.experimental import pallas as pl
from jax.experimental.pallas import tpu as pltpu
from jax.sharding import Mesh
from jax.sharding import PartitionSpec as P


LOW = 64
DEPTHS = 8
REPS = 4
SMALL = 8 * 1024 * 1024
CHUNK = 256
TOGETHER = 2
GRANT = 20 * 1024 * 1024
LANES = 128
BF = jnp.bfloat16
F32 = jnp.float32
I32 = jnp.int32
WHOLE = pl.BlockSpec(memory_space=pltpu.VMEM)
SCALARS = pl.BlockSpec(memory_space=pltpu.SMEM)


def two_parts(x):
    high = lax.reduce_precision(x, exponent_bits=8, mantissa_bits=7)
    return high.astype(BF), (x - high).astype(BF)


def finish_pool(sums, lengths_t):
    features, chips, width, lanes = sums.shape

    def kernel(x_ref, lengths_ref, out_ref):
        share = 1.0 / lengths_ref[pl.ds(pl.program_id(0), 1), :].astype(F32)
        total = x_ref[0]
        for chip in range(1, chips):
            total = total + x_ref[chip]
        out_ref[...] = total * share

    return pl.pallas_call(
        kernel,
        grid=(features,),
        in_specs=[
            pl.BlockSpec((None, chips, width, lanes), lambda i: (i, 0, 0, 0)),
            pl.BlockSpec((features, lanes), lambda i: (0, 0)),
        ],
        out_specs=pl.BlockSpec((None, width, lanes), lambda i: (i, 0, 0)),
        out_shape=jax.ShapeDtypeStruct((features, width, lanes), F32),
        compiler_params=pltpu.CompilerParams(vmem_limit_bytes=SMALL),
        name="finish_pool",
    )(sums, lengths_t)


def join(tops, bottoms):
    half, rows = tops[0].shape
    cols = rows // 2

    def kernel(*refs):
        out_ref = refs[-1]
        out_ref[0:half] = refs[0][...] + refs[1][...] + refs[2][...]
        out_ref[half:] = refs[3][...] + refs[4][...] + refs[5][...]

    spec = lambda n: pl.BlockSpec((n, cols), lambda i: (0, i))
    return pl.pallas_call(
        kernel,
        grid=(2,),
        in_specs=[spec(half)] * 6,
        out_specs=spec(2 * half),
        out_shape=jax.ShapeDtypeStruct((2 * half, rows), F32),
        compiler_params=pltpu.CompilerParams(vmem_limit_bytes=SMALL),
        name="join",
    )(*tops, *bottoms)


def estimate(width, rows, columns):
    flops = 4 * width * rows * columns
    return pl.CostEstimate(flops=flops, transcendentals=0, bytes_accessed=flops // 500)


def make_keys(base, rows_dev, ids_ref, key_low, key_high, key_count):
    bag = ids_ref.shape[1]
    own, low, lead = [], [], []
    for j in range(bag):
        ids = ids_ref[:, j, :]
        shifted = ids - base
        good = jnp.logical_and(ids >= 0, jnp.logical_and(shifted >= 0, shifted < rows_dev))
        own.append(jnp.where(good, shifted, -1))
        low.append(shifted & (LOW - 1))
        fresh = good
        for k in range(j):
            fresh = jnp.logical_and(fresh, own[k] != own[j])
        lead.append(fresh)
    deepest = jnp.zeros(own[0].shape, I32)
    for j in range(bag):
        count = jnp.ones(own[0].shape, F32)
        for k in range(j + 1, bag):
            count = count + jnp.where(own[k] == own[j], 1.0, 0.0)
        level = jnp.zeros(own[0].shape, I32)
        for k in range(j):
            level = level + jnp.where(jnp.logical_and(lead[k], low[k] == low[j]), 1, 0)
        key_low[j] = jnp.where(lead[j], low[j] + LOW * level, -1).astype(F32)
        key_high[j] = (own[j] >> (LOW.bit_length() - 1)).astype(F32)
        key_count[j] = count
        deepest = jnp.maximum(deepest, jnp.where(lead[j], level + 1, 0))
    return deepest


def spread(ref, j, source):
    return jnp.broadcast_to(ref[j, pl.ds(source, 1), :], (16, LANES)).astype(BF)


def first_layers(source, key_low, key_high, key_count):
    bag = key_low.shape[0]
    lows = [spread(key_low, j, source) for j in range(bag)]
    highs = [spread(key_high, j, source) for j in range(bag)]
    counts = [spread(key_count, j, source) for j in range(bag)]
    sub = lax.broadcasted_iota(I32, (16, LANES), 0).astype(F32)
    layers = []
    for depth in range(2):
        high_rows, count_rows = [], []
        for group in range(LOW // 16):
            place = (sub + float(LOW * depth + 16 * group)).astype(BF)
            high = jnp.full((16, LANES), -1.0, BF)
            count = jnp.zeros((16, LANES), BF)
            for j in range(bag):
                hit = lows[j] == place
                high = jnp.where(hit, highs[j], high)
                count = jnp.where(hit, counts[j], count)
            high_rows.append(high)
            count_rows.append(count)
        layers.append((jnp.concatenate(high_rows, axis=0), jnp.concatenate(count_rows, axis=0)))
    return layers


def deep_layer(source, depth, key_low, key_high, key_count):
    bag = key_low.shape[0]
    place = (lax.broadcasted_iota(I32, (LOW, LANES), 0) + LOW * depth).astype(F32)
    high = jnp.full((LOW, LANES), -1.0, F32)
    count = jnp.zeros((LOW, LANES), F32)
    for j in range(bag):
        hit = jnp.broadcast_to(key_low[j, pl.ds(source, 1), :], (LOW, LANES)) == place
        high = jnp.where(hit, jnp.broadcast_to(key_high[j, pl.ds(source, 1), :], (LOW, LANES)), high)
        count = jnp.where(hit, jnp.broadcast_to(key_count[j, pl.ds(source, 1), :], (LOW, LANES)), count)
    return high.astype(BF), count.astype(BF)


def counts_for(block, layers):
    want = jnp.asarray(block, F32).astype(BF)
    tile = jnp.zeros((LOW, LANES), BF)
    for high, count in layers:
        tile = jnp.where(high == want, count, tile)
    return tile


def pool_kernel(per_step, base_ref, ids_ref, upper_ref, lower_ref, out_ref, highs_ref, counts_ref, deep_ref,
                key_low, key_high, key_count):
    step = pl.program_id(0)
    width = out_ref.shape[1]
    rows_dev = upper_ref.shape[1]
    sources = ids_ref.shape[0]

    def build(at):
        for s in range(per_step):
            layers = first_layers(at * per_step + s, key_low, key_high, key_count)
            for depth in range(2):
                highs_ref[depth, at * per_step + s] = layers[depth][0]
                counts_ref[depth, at * per_step + s] = layers[depth][1]

    @pl.when(step == 0)
    def _():
        deepest = make_keys(base_ref[0], rows_dev, ids_ref, key_low, key_high, key_count)
        deep_ref[0] = 0
        source_of = lax.broadcasted_iota(I32, deepest.shape, 0)
        code = jnp.where(deepest > 2, source_of * 16 + deepest, 0)

        def note_all(top):
            source = top // 16

            def note(depth, carry):
                deep_ref[0] += 1
                deep_ref[deep_ref[0]] = source * DEPTHS + depth
                return carry

            lax.fori_loop(2, top % 16, note, 0)
            return jnp.max(jnp.where(source_of < source, code, 0))

        lax.while_loop(lambda top: top > 0, note_all, jnp.max(code))

        build(0)

    layers = [[(highs_ref[depth, step * per_step + s], counts_ref[depth, step * per_step + s])
               for depth in range(2)] for s in range(per_step)]
    both = lambda cols: jnp.concatenate([upper_ref[:, cols], lower_ref[:, cols]], axis=0)
    chunk = CHUNK
    total = jnp.zeros((2 * width, LANES * per_step), F32)
    for c in range(0, rows_dev, chunk):
        tile = jnp.concatenate(
            [jnp.concatenate([counts_for(c // LOW + h, layers[s]) for h in range(chunk // LOW)], axis=0)
             for s in range(per_step)], axis=1)
        total = total + jnp.dot(both(slice(c, c + chunk)), tile, preferred_element_type=F32)
    for s in range(per_step):
        cols = slice(LANES * s, LANES * (s + 1))
        out_ref[s] = total[0:width, cols] + total[width : 2 * width, cols]

    build(jnp.minimum(step + 1, sources // per_step - 1))

    def deeper(entry, carry):
        source = deep_ref[1 + entry] // DEPTHS

        @pl.when(source // per_step == step)
        def _():
            extra = deep_layer(source, deep_ref[1 + entry] % DEPTHS, key_low, key_high, key_count)
            wide = 1024

            def add(block, value):
                tile = jnp.concatenate([counts_for(block * (wide // LOW) + h, [extra])
                                        for h in range(wide // LOW)], axis=0)
                return value + jnp.dot(both(pl.ds(pl.multiple_of(block * wide, wide), wide)),
                                       tile, preferred_element_type=F32)

            more = lax.fori_loop(0, rows_dev // wide, add, jnp.zeros((2 * width, LANES), F32))
            out_ref[source % per_step] += more[0:width] + more[width : 2 * width]

        return carry

    lax.fori_loop(0, deep_ref[0], deeper, 0)


def pool(base, ids, parts):
    sources, bag, _ = ids.shape
    width, rows_dev = parts[0].shape
    per_step = 2
    keys = jax.ShapeDtypeStruct((bag, sources, LANES), F32)
    layer = jax.ShapeDtypeStruct((2, sources, LOW, LANES), BF)
    return pl.pallas_call(
        functools.partial(pool_kernel, per_step),
        grid=(sources // per_step,),
        in_specs=[SCALARS, WHOLE, WHOLE, WHOLE],
        out_specs=[pl.BlockSpec((per_step, width, LANES), lambda i: (i, 0, 0)), WHOLE, WHOLE, SCALARS, WHOLE, WHOLE, WHOLE],
        out_shape=[
            jax.ShapeDtypeStruct((sources, width, LANES), F32),
            layer,
            layer,
            jax.ShapeDtypeStruct((1 + sources * DEPTHS,), I32),
            keys,
            keys,
            keys,
        ],
        compiler_params=pltpu.CompilerParams(dimension_semantics=("arbitrary",), vmem_limit_bytes=GRANT),
        cost_estimate=estimate(width, rows_dev, sources * LANES),
        name="pool",
    )(base, ids, *parts)


def grad_kernel(blk, steps, aheads, rep_ref, *refs):
    halves, outs = [refs[0:8], refs[8:16]], refs[16:]
    width = halves[0][0].shape[1]
    step = pl.program_id(0)
    groups = len(aheads)
    ahead = jnp.where(step < steps, aheads[0], aheads[-1])
    start = ((rep_ref[0] + ahead) & (REPS - 1)) * (steps * blk // LOW) + step % steps * (blk // LOW)
    together = TOGETHER
    total = jnp.zeros((2 * width, blk), F32)
    for upper_ref, lower_ref, highs_ref, counts_ref, deep_ref, *keys in halves:
        for s in range(0, upper_ref.shape[0], together):
            tile = jnp.concatenate(
                [jnp.concatenate([counts_for(start + h, [(highs_ref[d, s + t], counts_ref[d, s + t]) for d in range(2)])
                                  for h in range(blk // LOW)], axis=0)
                 for t in range(together)], axis=1)
            lhs = jnp.concatenate([jnp.concatenate([upper_ref[s + t], lower_ref[s + t]], axis=0)
                                   for t in range(together)], axis=1)
            total = total + lax.dot_general(lhs, tile,
                                            (((1,), (1,)), ((), ())), preferred_element_type=F32)

    def put(value, more):
        each = len(outs) // groups
        for group in range(groups):
            @pl.when(step // steps == group)
            def _():
                for part in range(each):
                    ref, at = outs[each * group + part], part * (width // each)
                    new = value[at : at + width // each] + value[width + at : width + at + width // each]
                    ref[...] = ref[...] + new if more else new

    put(total, False)

    for upper_ref, lower_ref, highs_ref, counts_ref, deep_ref, *keys in halves:
        def deeper(entry, carry, upper_ref=upper_ref, lower_ref=lower_ref, deep_ref=deep_ref, keys=keys):
            s = deep_ref[1 + entry] // DEPTHS
            extra = deep_layer(s, deep_ref[1 + entry] % DEPTHS, *keys)
            tile = jnp.concatenate([counts_for(start + h, [extra]) for h in range(blk // LOW)], axis=0)
            lhs = jnp.concatenate([upper_ref[s], lower_ref[s]], axis=0)
            put(lax.dot_general(lhs, tile, (((1,), (1,)), ((), ())), preferred_element_type=F32), True)
            return carry

        lax.fori_loop(0, deep_ref[0], deeper, 0)


def grads(rep, aheads, each, rows, own, other):
    sources, width, _ = own[0].shape
    blk = 1024
    steps = rows // blk
    outs = [pl.BlockSpec((width // each, blk), lambda i, g=g: (0, jnp.clip(i - g * steps, 0, steps - 1)))
            for g in range(len(aheads)) for _ in range(each)]
    side = [WHOLE, WHOLE, WHOLE, WHOLE, SCALARS, WHOLE, WHOLE, WHOLE]
    return pl.pallas_call(
        functools.partial(grad_kernel, blk, steps, aheads),
        grid=(steps * len(aheads),),
        in_specs=[SCALARS] + side + side,
        out_specs=outs,
        out_shape=[jax.ShapeDtypeStruct((width // each, rows), F32)] * len(outs),
        compiler_params=pltpu.CompilerParams(dimension_semantics=("arbitrary",), vmem_limit_bytes=GRANT),
        cost_estimate=estimate(width, rows * len(aheads), 2 * sources * LANES),
        name="grads",
    )(rep, *own, *other)


def to_all(x, axis):
    return lax.all_to_all(x, axis, split_axis=0, concat_axis=0, tiled=True)


def shifted(x, axis, by):
    n = lax.axis_size(axis)
    return lax.ppermute(x, axis, [(i, (i + by) % n) for i in range(n)])


def inner(emb_table, feature_ids, lengths, cotangent):
    rows_dev, width = emb_table.shape
    examples, features, bag = feature_ids.shape
    chips = lax.axis_size("x")
    cores = lax.axis_size("core")
    reps = lax.axis_size("rep")
    core = lax.axis_index("core")
    rep = lax.axis_index("rep")
    base = ((lax.axis_index("x") * cores + core) * rows_dev).astype(I32).reshape(1)

    ids_t = jnp.transpose(feature_ids, (1, 2, 0))
    lengths_t = jnp.transpose(lengths, (1, 0))
    share = 1.0 / lengths_t.astype(F32)
    slot = lax.broadcasted_iota(I32, ids_t.shape, 1)
    masked = jnp.where(slot < lengths_t[:, None, :], ids_t, -1)
    spread_ids = jnp.repeat(masked, chips * cores, axis=0)
    ids = to_all(spread_ids, ("z", "x", "core"))
    parts = two_parts(jnp.transpose(emb_table))
    ids = ids.reshape(features * chips, cores, bag, examples)
    ids_own = lax.dynamic_index_in_dim(ids, core, 1, keepdims=False)
    ids_other = lax.dynamic_index_in_dim(ids, 1 - core, 1, keepdims=False)

    scaled = jnp.transpose(cotangent, (1, 2, 0)) * share[:, None, :]
    spread_cot = jnp.broadcast_to(scaled[:, None], (features, chips, width, examples))
    spread_cot = spread_cot.reshape(features * chips, width, examples)
    scaled_own = to_all(spread_cot, ("z", "x"))
    scaled_other = shifted(scaled_own, "core", 1)

    sent, *layers_other = pool(base, ids_other, parts)
    sent = shifted(sent, "core", 1)
    kept, *layers_own = pool(base, ids_own, parts)
    pooled = to_all(kept + sent, ("z", "x")).reshape(features, chips, width, examples)
    pooled = finish_pool(pooled, lengths_t)

    own = [*two_parts(scaled_own), *layers_own]
    other = [*two_parts(scaled_other), *layers_other]
    rows = rows_dev // reps

    def blocks(*ahead):
        return grads(rep.astype(I32).reshape(1), ahead, 2, rows, own, other)

    far_top, far_bottom = blocks(2)
    from_left = shifted(far_top, "rep", 1)
    from_right = shifted(far_bottom, "rep", -1)
    next_top, next_bottom, prev_top, prev_bottom = blocks(1, reps - 1)
    got_bottom = shifted(next_bottom, "rep", 1)
    got_top = shifted(prev_top, "rep", -1)
    got_left_top = shifted(next_top + from_left, "rep", 1)
    got_right_bottom = shifted(prev_bottom + from_right, "rep", -1)
    here_top, here_bottom = blocks(0)
    row_grads = join([here_top, got_top, got_left_top], [here_bottom, got_bottom, got_right_bottom])
    return jnp.transpose(pooled, (2, 0, 1)), jnp.transpose(row_grads)


def solution(mesh):
    devices = mesh.devices.reshape(4, 4, 2, mesh.shape["rep"])
    fine = Mesh(devices, ("z", "x", "core", "rep"))
    dev = ("z", "x", "core")
    every = ("z", "x", "core", "rep")
    return jax.shard_map(
        inner,
        mesh=fine,
        in_specs=(P(dev, None), P(every, None, None), P(every, None), P(every, None, None)),
        out_specs=(P(every, None, None), P(every, None)),
        check_vma=False,
    )
```
